512 devices in a mesh: rows: 32 (over z, x), seq: 16 (over y, core).
Axes of the slice: x: 4, y: 8, z: 8, core: 2. Of those that a mesh axis runs over, the one named last changes fastest.
Arguments:
- qkv: bfloat16 [32, 1024, 3840], P('rows', 'seq'), may hold values from -24 to 24
- hidden: bfloat16 [32, 1024, 1280], P('rows', 'seq'), may hold values from -3 to 3
- segment_ids: int32 [32, 1024], P('rows', 'seq'), may hold values from 0 to 4, as said below
- key_keep: int32 [32, 1024], P('rows', 'seq'), may hold values 0 or 1
- grid_sizes: int32 [32, 4, 2], P('rows'), may hold values from 8 to 16, as said below
- owner_slots: int32 [32, 4], P('rows'), may hold values from 0 to 15, as said below
- out_weight: bfloat16 [1280, 1280], P('rows'), may hold values from -0.15625 to 0.15625
- norm_gain: float32 [1280], replicated, may hold values from 0.5 to 1.5
- norm_bias: float32 [1280], replicated, may hold values from -1.5 to 1.5
- merge_weight: bfloat16 [5120, 4096], P(None, 'seq'), may hold values from -0.078125 to 0.078125
Outputs:
- normed: bfloat16 [32, 1024, 1280], P('rows', 'seq')
- request_norm: float32 [32, 16], P('rows', 'seq')
- request_peak: float32 [32, 16], P('rows', 'seq')
The draws below stay inside these ranges and needn't reach their ends.
Inputs may be any that keep to these rules, and one draw needn't show every extreme that they name: `segment_ids`: segment ids never fall along a pack: image j covers h_j w_j tokens right after image j - 1, and tokens after the last image carry 4; every pack ends with some such padding. Inside an image each aligned group of 4 tokens is one 2 x 2 block of the patch grid, blocks in row-major order. `grid_sizes`: both sides are even; rows run from 8 to 16, columns from 8 to 14; the first image of every pack has 16 rows and 14 columns; the images of a pack agree with segment_ids. `owner_slots`: the images of one pack have distinct slots.
All inputs are finite; a program needn't handle non-finite values. No bound on the sum of `key_keep` on one device may be relied on, other than what follows from the above.
Results may differ from the reference program's by a relative error of at most 0.0057.
Values may be sent and summed in bfloat16 or wider, within the bound.
No kernel may reach another device: no remote copies, remote signals or barrier semaphores. Data moves between devices by JAX's collectives and lax.ppermute only.
A program may use at most 64 MiB of HBM per device.

```python
import jax
import jax.numpy as jnp
from jax import lax

D = 1280
HEADS = 16
HD = 80
OUT = 4096
GRID = 16
PACKS = 32
SEQ_LEN = 1024
IMGS = 4
SLOTS = 16


def grid_helper(key):
    row_key = jax.random.fold_in(key, 11)
    col_key = jax.random.fold_in(key, 13)
    row_sides = 2 * jax.random.randint(row_key, (PACKS, IMGS), GRID // 4, GRID // 2 + 1)
    col_sides = 2 * jax.random.randint(col_key, (PACKS, IMGS), GRID // 4, GRID // 2)
    leading = jnp.arange(IMGS)[None, :] == 0
    row_sides = jnp.where(leading, GRID, row_sides)
    col_sides = jnp.where(leading, GRID - 2, col_sides)
    return jnp.stack([row_sides, col_sides], axis=2).astype(jnp.int32)


def draw_grid_sizes(key, part):
    return grid_helper(key)


def draw_segment_ids(key, part):
    patch_grid = grid_helper(key)
    lengths = patch_grid[:, :, 0] * patch_grid[:, :, 1]
    ends = jnp.cumsum(lengths, axis=1)
    places = jnp.arange(SEQ_LEN, dtype=jnp.int32)
    passed = places[None, :, None] >= ends[:, None, :]
    return jnp.sum(passed.astype(jnp.int32), axis=2).astype(jnp.int32)


def draw_owner_slots(key, part):
    pack_keys = jax.random.split(jax.random.fold_in(key, 23), PACKS)
    shuffled = jax.vmap(lambda pack_key: jax.random.permutation(pack_key, SLOTS))(pack_keys)
    return shuffled[:, :IMGS].astype(jnp.int32)


def draw_qkv(key, part):
    shape = (PACKS, SEQ_LEN, 3, HEADS, HD)
    base = jax.random.normal(key, shape, jnp.float32)
    factor = jnp.array([1.0, 1.0, 2.5], jnp.float32)[None, None, :, None, None]
    base = base * factor
    return jnp.clip(base, -24.0, 24.0).reshape(PACKS, SEQ_LEN, 3 * HEADS * HD).astype(jnp.bfloat16)


def with_ends(entries, rng, least, high):
    longest = entries.shape.index(max(entries.shape))
    spots = []
    for shift in (0, 1):
        where = [jax.random.randint(jax.random.fold_in(rng, axis), (), 0, length) for axis, length in enumerate(entries.shape)]
        where[longest] = (where[longest] + shift) % entries.shape[longest]
        spots.append(tuple(where))
    return entries.at[spots[0]].set(least).at[spots[1]].set(high)


def steps_of(stream_key, dims, cuts, least, top_value):
    loudness = 1.0
    for dim, shards_of in cuts:
        heights = jax.random.uniform(jax.random.fold_in(jax.random.fold_in(stream_key, 6), dim), (shards_of,), jnp.float32, least / len(cuts), top_value / len(cuts))
        loudness = loudness * jnp.repeat(jnp.exp(heights), dims[dim] // shards_of).reshape((-1,) + (1,) * (len(dims) - 1 - dim))
    return loudness


def normal_values(own_key, extent, width, reach, shards=(), kind=jnp.bfloat16):
    result = width * jax.random.normal(own_key, extent, jnp.float32)
    if shards:
        result = result * steps_of(own_key, extent, shards, -0.22, 0.18)
    return jnp.clip(result, -reach, reach).astype(kind)


def setup_inputs(seed: int = 0) -> dict:
    key_of = jax.random.split(jax.random.key(seed), 11)
    return {
        "qkv": draw_qkv(jax.random.fold_in(key_of[10], 71), 0),
        "hidden": normal_values(key_of[1], (PACKS, SEQ_LEN, D), 0.5, 3.0, ((0, 32), (1, 16))),
        "segment_ids": draw_segment_ids(jax.random.fold_in(key_of[10], 71), 0),
        "key_keep": with_ends((jax.random.randint(key_of[3], (PACKS, SEQ_LEN), 0, 8) < 7).astype(jnp.int32), jax.random.fold_in(key_of[3], 1), 0, 1),
        "grid_sizes": draw_grid_sizes(jax.random.fold_in(key_of[10], 71), 0),
        "owner_slots": draw_owner_slots(jax.random.fold_in(key_of[10], 71), 0),
        "out_weight": normal_values(key_of[6], (D, D), D ** -0.5, 0.15625, ((0, 32),)),
        "norm_gain": jnp.clip(1.0 + 0.1 * jax.random.normal(key_of[7], (D,), jnp.float32), 0.5, 1.5),
        "norm_bias": normal_values(key_of[8], (D,), 0.3, 1.5, (), jnp.float32),
        "merge_weight": normal_values(key_of[9], (4 * D, OUT), (4 * D) ** -0.5, 0.078125, ((1, 16),)),
    }


def positions(segment, places, patch_grid):
    image_count = patch_grid.shape[0]
    widths = patch_grid[:, 1]
    lengths = patch_grid[:, 0] * widths
    starts = jnp.cumsum(lengths) - lengths
    is_valid = segment < image_count
    image_hot = segment[:, None] == jnp.arange(image_count, dtype=jnp.int32)[None, :]
    begins = lax.optimization_barrier(jnp.sum(jnp.where(image_hot, starts[None, :], 0), axis=1))
    token_width = jnp.maximum(lax.optimization_barrier(jnp.sum(jnp.where(image_hot, widths[None, :], 0), axis=1)), 2)
    offset = places - begins
    square = offset // 4
    corner = offset % 4
    half_width = token_width // 2
    row_pos = 2 * (square // half_width) + corner // 2
    col_pos = 2 * (square % half_width) + corner % 2
    row_pos = jnp.where(is_valid, row_pos, 0).astype(jnp.int32)
    col_pos = jnp.where(is_valid, col_pos, 0).astype(jnp.int32)
    return (row_pos, col_pos)

def rotary(values, row_pos, col_pos):
    quarter = values.shape[-1] // 4
    rates = 10000.0 ** (-jnp.arange(quarter, dtype=jnp.float32) / quarter)

    def rotate_pair(part, place):
        angle = place.astype(jnp.float32)[:, None] * rates[None, :]
        cosine = jnp.cos(angle)[:, None, :]
        sine = jnp.sin(angle)[:, None, :]
        first_half = part[..., :quarter]
        second_half = part[..., quarter:]
        return jnp.concatenate([first_half * cosine - second_half * sine, second_half * cosine + first_half * sine], axis=-1)
    middle = 2 * quarter
    return jnp.concatenate([rotate_pair(values[..., :middle], row_pos), rotate_pair(values[..., middle:], col_pos)], axis=-1)

def layer_norm(mixed, norm_gain, norm_bias):
    row_mean = lax.optimization_barrier(jnp.mean(mixed, axis=-1, keepdims=True))
    centred = mixed - row_mean
    spread = lax.optimization_barrier(jnp.mean(centred * centred, axis=-1, keepdims=True))
    return (centred * lax.rsqrt(spread + 1e-05) * norm_gain + norm_bias).astype(jnp.bfloat16)

def slot_counts(patch_grid, owner, slot_total):
    quads = patch_grid[:, 0] * patch_grid[:, 1] // 4
    owner_hot = owner[:, None] == jnp.arange(slot_total, dtype=jnp.int32)[None, :]
    return lax.optimization_barrier(jnp.sum(jnp.where(owner_hot, quads[:, None], 0), axis=0))

def reference(qkv, hidden, segment_ids, key_keep, grid_sizes, owner_slots, out_weight, norm_gain, norm_bias, merge_weight):
    score_scale = HD ** (-0.5)

    def one_pack(inputs):
        pack_qkv, pack_hidden, segment, key_flags, patch_grid, owner = inputs
        places = jnp.arange(SEQ_LEN, dtype=jnp.int32)
        row_pos, col_pos = positions(segment, places, patch_grid)
        split = pack_qkv.reshape(SEQ_LEN, 3, HEADS, HD)
        queries = rotary(split[:, 0].astype(jnp.float32), row_pos, col_pos).astype(jnp.bfloat16)
        key_rows = rotary(split[:, 1].astype(jnp.float32), row_pos, col_pos).astype(jnp.bfloat16)
        value_rows = split[:, 2]
        same_image = (segment[:, None] == segment[None, :]) & (segment[:, None] < IMGS) & (key_flags[None, :] == 1)
        allowed = same_image | (places[:, None] == places[None, :])

        def one_head(head_inputs):
            query_head, key_head, value_head = head_inputs
            scores = jnp.dot(query_head, key_head.T, preferred_element_type=jnp.float32) * score_scale
            top = lax.optimization_barrier(jnp.max(jnp.where(allowed, scores, -1e+30), axis=1, keepdims=True))
            weights = jnp.where(allowed, jnp.exp(scores - top), 0.0)
            totals = lax.optimization_barrier(jnp.sum(weights, axis=1, keepdims=True))
            summed = jnp.dot(weights.astype(jnp.bfloat16), value_head, preferred_element_type=jnp.float32)
            return (summed / totals).astype(jnp.bfloat16)
        head_out = lax.map(one_head, (jnp.transpose(queries, (1, 0, 2)), jnp.transpose(key_rows, (1, 0, 2)), jnp.transpose(value_rows, (1, 0, 2))))
        attended = jnp.transpose(head_out, (1, 0, 2)).reshape(SEQ_LEN, D)
        mixed = pack_hidden.astype(jnp.float32) + jnp.dot(attended, out_weight, preferred_element_type=jnp.float32)
        normed = layer_norm(mixed, norm_gain, norm_bias)
        merged = normed.reshape(SEQ_LEN // 4, 4 * D)
        projected = jnp.dot(merged, merge_weight, preferred_element_type=jnp.float32)
        squares = lax.optimization_barrier(jnp.sum(projected * projected, axis=1))
        peaks = lax.optimization_barrier(jnp.max(projected, axis=1))
        merge_image = segment[::4]
        is_valid = merge_image < IMGS
        image_hot = merge_image[:, None] == jnp.arange(IMGS, dtype=jnp.int32)[None, :]
        merge_slot = lax.optimization_barrier(jnp.sum(jnp.where(image_hot, owner[None, :], 0), axis=1))
        slot_hot = (merge_slot[:, None] == jnp.arange(SLOTS, dtype=jnp.int32)[None, :]) & is_valid[:, None]
        slot_sums = lax.optimization_barrier(jnp.sum(jnp.where(slot_hot, squares[:, None], 0.0), axis=0))
        slot_tops = lax.optimization_barrier(jnp.max(jnp.where(slot_hot, peaks[:, None], -1e+30), axis=0))
        counts = slot_counts(patch_grid, owner, SLOTS)
        present = counts > 0
        divisor = (jnp.maximum(counts, 1) * OUT).astype(jnp.float32)
        norm_out = jnp.where(present, jnp.sqrt(slot_sums / divisor + 1e-06), 0.0)
        peak_out = jnp.where(present, slot_tops, 0.0)
        return (normed, norm_out, peak_out)
    normed, norm_out, peak_out = lax.map(one_pack, (qkv, hidden, segment_ids, key_keep, grid_sizes, owner_slots))
    return (normed, norm_out, peak_out)
```

```python
import functools

import jax
import jax.numpy as jnp
import numpy as np
from jax import lax
from jax.experimental import pallas as pl
from jax.experimental.pallas import tpu as pltpu
from jax.sharding import PartitionSpec as P

D = 1280
HEADS = 16
HD = 80
OUT = 4096
IMGS = 4
SEQ = 1024
TOK = 64
CHIPS = 8
MAXIMG = 896
NEG = -1e30


F32 = jnp.float32
BF16 = jnp.bfloat16
VM = pl.BlockSpec(memory_space=pltpu.VMEM)
SM = pl.BlockSpec(memory_space=pltpu.SMEM)


def iota(shape, dim):
    return lax.broadcasted_iota(jnp.int32, shape, dim)


def image_bounds(grid_ref):
    starts, ends, total = [], [], 0
    for j in range(IMGS):
        starts.append(total)
        total = total + grid_ref[j, 0] * grid_ref[j, 1]
        ends.append(total)
    return starts, ends


def rotary_kernel(me_ref, grid_ref, keep_ref, rate_ref, qkv_ref, out_ref):
    starts, ends = image_bounds(grid_ref)
    place = me_ref[0] * TOK + iota((TOK, 256), 0)
    begin = jnp.zeros((TOK, 256), jnp.int32)
    width = jnp.full((TOK, 256), 2, jnp.int32)
    for j in range(IMGS):
        inside = (place >= starts[j]) & (place < ends[j])
        begin = jnp.where(inside, starts[j], begin)
        width = jnp.where(inside, grid_ref[j, 1], width)
    valid = place < ends[IMGS - 1]
    offset = place - begin
    square = lax.shift_right_logical(offset, 2)
    corner = offset & 3
    half = lax.shift_right_logical(width, 1)
    line = jnp.floor((square.astype(F32) + 0.5) / half.astype(F32)).astype(jnp.int32)
    row = 2 * line + lax.shift_right_logical(corner, 1)
    col = 2 * (square - line * half) + (corner & 1)
    row = jnp.where(valid, row, 0).astype(F32)
    col = jnp.where(valid, col, 0).astype(F32)
    lane = iota((TOK, 256), 1) & 127
    rotated = lane < HD
    angle = jnp.where(lane < HD // 2, row, col) * rate_ref[0:1, :]
    cosine = jnp.where(rotated, jnp.cos(angle), 1.0)
    low = (lane < 20) | ((lane >= 40) & (lane < 60))
    sine = jnp.sin(angle)
    sine = jnp.where(rotated, jnp.where(low, -sine, sine), 0.0)
    tail = jnp.broadcast_to(keep_ref[:, 0:1], (TOK, 128)).astype(F32)[:, :16]
    for dest in range(HEADS):
        q = qkv_ref[:, dest * HD : dest * HD + HD].astype(F32)
        k = qkv_ref[:, D + dest * HD : D + dest * HD + HD].astype(F32)
        v = qkv_ref[:, 2 * D + dest * HD : 2 * D + dest * HD + HD].astype(F32)
        full = jnp.concatenate([q, v[:, :48], k, v[:, 48:], tail], axis=1)
        swapped = jnp.where(low, pltpu.roll(full, 256 - 20, 1), pltpu.roll(full, 20, 1))
        out_ref[dest] = (full * cosine + swapped * sine).astype(BF16)


def attention_kernel(grid_ref, x_ref, out_ref):
    starts, ends = image_bounds(grid_ref)
    pick = jnp.where(iota((8, 128), 1) == 112, 1.0, 0.0).astype(BF16)
    keep = lax.dot_general(
        pick, x_ref[:, 128:], (((1,), (1,)), ((), ())), preferred_element_type=F32
    )[0:1]
    key_place = jnp.where(keep > 0.5, iota((1, SEQ), 1), -1)
    query_lane = iota((128, 128), 1) < HD

    def emit(chip, rows):
        flipped = jnp.transpose(rows)
        out_ref[chip] = jnp.concatenate(
            [flipped[80:128], flipped[208:240]], axis=0
        ).astype(BF16)

    for chip in range(MAXIMG // 128):
        first = chip * 128
        low = max(0, first - 256)
        high = min(MAXIMG, first + 384)
        query = jnp.where(query_lane, x_ref[first : first + 128, 0:128], 0)
        scores = lax.dot_general(
            query,
            x_ref[low:high, 128:256],
            (((1,), (1,)), ((), ())),
            preferred_element_type=F32,
        ) * HD ** (-0.5)
        place = first + iota((128, 1), 0)
        lo = place
        hi = place
        for j in range(IMGS):
            inside = (place >= starts[j]) & (place < ends[j])
            lo = jnp.where(inside, starts[j], lo)
            hi = jnp.where(inside, ends[j], hi)
        keys = key_place[:, low:high]
        same = (keys >= lo) & (keys < hi)
        own = iota((1, high - low), 1) + low == place
        scores = jnp.where(same | own, scores, NEG)
        top = jnp.max(scores, axis=1, keepdims=True)
        weights = jnp.exp(scores - top)
        total = jnp.sum(weights, axis=1, keepdims=True)
        summed = jnp.dot(
            weights.astype(BF16), x_ref[low:high, :], preferred_element_type=F32
        )
        emit(chip, summed / total)
    emit(CHIPS - 1, x_ref[MAXIMG:SEQ, :].astype(F32))


def mix_kernel(core_ref, heads_ref, weight_ref, hidden_ref, own_ref, send_ref, part_ref):
    part_ref[...] = lax.dot_general(
        heads_ref[...],
        weight_ref[...],
        (((0,), (0,)), ((), ())),
        preferred_element_type=F32,
    )
    core = core_ref[0]
    mine = pl.multiple_of(core * TOK, TOK)
    other = pl.multiple_of((1 - core) * TOK, TOK)
    own_ref[...] = part_ref[pl.ds(mine, TOK), :] + hidden_ref[...].astype(F32)
    send_ref[...] = part_ref[pl.ds(other, TOK), :]


def norm_kernel(own_ref, recv_ref, gain_ref, bias_ref, normed_ref, block_ref):
    mixed = own_ref[...] + recv_ref[...]
    centred = mixed - jnp.mean(mixed, axis=1, keepdims=True)
    spread = jnp.mean(centred * centred, axis=1, keepdims=True)
    normed = centred * lax.rsqrt(spread + 1e-05) * gain_ref[...] + bias_ref[...]
    normed = normed.astype(BF16)
    normed_ref[...] = normed
    line = iota((TOK, TOK), 0)
    source = 4 * (line & 15) + lax.shift_right_logical(line, 4)
    order = jnp.where(iota((TOK, TOK), 1) == source, 1.0, 0.0).astype(BF16)
    block_ref[...] = jnp.dot(order, normed, preferred_element_type=F32).astype(BF16)


def project_kernel(me_ref, grid_ref, owner_ref, wa_ref, wb_ref, *refs):
    blocks = refs[:CHIPS]
    out_ref = refs[CHIPS]
    acc_ref = refs[CHIPS + 1]
    corner = pl.program_id(0)
    first = pl.multiple_of(corner * 16, 16)
    rows = jnp.concatenate([b[pl.ds(first, 16), :] for b in blocks], axis=0)
    part = jnp.concatenate(
        [
            jnp.dot(rows, wa_ref[...], preferred_element_type=F32),
            jnp.dot(rows, wb_ref[...], preferred_element_type=F32),
        ],
        axis=1,
    )

    @pl.when(corner == 0)
    def _():
        acc_ref[...] = part

    @pl.when(corner > 0)
    def _():
        acc_ref[...] += part

    @pl.when(corner == 3)
    def _():
        done = acc_ref[...]
        squares = jnp.sum(done * done, axis=1, keepdims=True)
        peaks = jnp.max(done, axis=1, keepdims=True)
        _, ends = image_bounds(grid_ref)
        me = me_ref[0]
        line = iota((128, 128), 0)
        step = lax.shift_right_logical(line, 4)
        shift = lax.shift_right_logical(step + 1, 1)
        shift = jnp.where((step & 1) == 1, -shift, shift)
        source = (me + 2 * shift) & 15
        token = source * TOK + 4 * (line & 15)
        slot = jnp.full((128, 128), -1, jnp.int32)
        for j in reversed(range(IMGS)):
            slot = jnp.where(token < ends[j], owner_ref[j], slot)
        hot = slot == iota((128, 128), 1)
        sums = jnp.sum(jnp.where(hot, squares, 0.0), axis=0, keepdims=True)
        tops = jnp.max(jnp.where(hot, peaks, NEG), axis=0, keepdims=True)
        both = jnp.where(line == 0, sums, jnp.where(line == 1, tops, 0.0))
        out_ref[...] = jnp.transpose(both)[:16]


def final_kernel(me_ref, grid_ref, owner_ref, stats_ref, out_ref):
    stats = stats_ref[...]
    total = jnp.sum(stats, axis=0, keepdims=True)
    top = jnp.max(stats, axis=0, keepdims=True)
    me = me_ref[0]
    count = 0
    for j in range(IMGS):
        size = lax.shift_right_logical(grid_ref[j, 0] * grid_ref[j, 1], 2)
        count = count + jnp.where(owner_ref[j] == me, size, 0)
    counts = jnp.full((1, 128), count, jnp.int32)
    divisor = (jnp.maximum(counts, 1) * OUT).astype(F32)
    norm = jnp.sqrt(total / divisor + 1e-06)
    lane = iota((1, 128), 1)
    both = jnp.where(lane == 0, norm, top)
    out_ref[...] = jnp.broadcast_to(jnp.where(counts > 0, both, 0.0), (8, 128))


def call(kernel, out, specs, scratch=(), flops=0, bytes_accessed=0, **kw):
    many = isinstance(out, (tuple, list))
    return pl.pallas_call(
        kernel,
        out_shape=out,
        in_specs=specs,
        out_specs=tuple([VM] * len(out)) if many else VM,
        scratch_shapes=scratch,
        cost_estimate=pl.CostEstimate(
            flops=flops, bytes_accessed=bytes_accessed, transcendentals=0
        ),
        **kw,
    )


def shape(dims, dtype):
    return jax.ShapeDtypeStruct(dims, dtype)


def chip_shift(x, step, flip=0):
    pairs = []
    for s in range(2 * CHIPS):
        chip, core = s // 2, s % 2
        pairs.append((s, ((chip + step) % CHIPS) * 2 + (core ^ flip)))
    return lax.ppermute(x, "seq", pairs)


def gather_weight(weight):
    def shift_x(step):
        pairs = []
        for r in range(32):
            z, x = r // 4, r % 4
            for s in range(16):
                if (x - 2 * (s % 2)) % 4 < 2:
                    pairs.append((r * 16 + s, (z * 4 + (x + step) % 4) * 16 + s))
        return lax.ppermute(weight, ("rows", "seq"), pairs)

    plus, minus, two = shift_x(1), shift_x(-1), shift_x(2)
    rel = (lax.axis_index("rows") - 2 * (lax.axis_index("seq") % 2)) % 4

    def pick(a, b, c, d):
        return jnp.where(
            rel == 0, a, jnp.where(rel == 1, b, jnp.where(rel == 2, c, d))
        )

    pair = jnp.concatenate(
        [pick(weight, plus, two, minus), pick(minus, weight, plus, two)], axis=0
    )
    groups = [[z * 4 + x for z in range(8)] for x in range(4)]
    spread = jnp.broadcast_to(pair[None], (8, 80, D))
    return lax.all_to_all(
        spread, "rows", split_axis=0, concat_axis=0, axis_index_groups=groups, tiled=True
    ).reshape(640, D)


def body(
    qkv,
    hidden,
    segment_ids,
    key_keep,
    grid_sizes,
    owner_slots,
    out_weight,
    norm_gain,
    norm_bias,
    merge_weight,
):
    del segment_ids
    me = lax.axis_index("seq").astype(jnp.int32)
    me1 = me.reshape(1)
    grid = grid_sizes[0]
    owner = owner_slots[0]
    base = np.float32(10000.0) ** (-(np.arange(20, dtype=np.float32) / np.float32(20)))
    rate = np.zeros((128,), np.float32)
    for part in range(4):
        rate[20 * part : 20 * part + 20] = base
    rate = jnp.asarray(np.broadcast_to(np.concatenate([rate, rate])[None], (8, 256)))
    keep = key_keep[0].reshape(TOK, 1)
    packed = call(
        rotary_kernel,
        shape((HEADS, TOK, 256), BF16),
        [SM, SM, VM, VM, VM],
        flops=1 << 22,
        bytes_accessed=1 << 20,
    )(me1, grid, keep, rate, qkv[0])
    heads_all = lax.all_to_all(packed, "seq", split_axis=0, concat_axis=0, tiled=True)
    weight = gather_weight(out_weight)
    merge_other = chip_shift(merge_weight, 0, 1)
    head_out = call(
        attention_kernel,
        shape((CHIPS, HD, 128), BF16),
        [SM, VM],
        flops=1 << 29,
        bytes_accessed=1 << 20,
    )(grid, heads_all.reshape(SEQ, 256))
    groups = [[2 * c + p for c in range(CHIPS)] for p in range(2)]
    attended = lax.all_to_all(
        head_out, "seq", split_axis=0, concat_axis=0, axis_index_groups=groups, tiled=True
    ).reshape(640, 128)
    own, send = call(
        mix_kernel,
        (shape((TOK, D), F32), shape((TOK, D), F32)),
        [SM, VM, VM, VM],
        scratch=[pltpu.VMEM((128, D), F32)],
        flops=1 << 28,
        bytes_accessed=3 << 20,
    )(me1 % 2, attended, weight, hidden[0])
    recv = chip_shift(send, 0, 1)
    normed, block = call(
        norm_kernel,
        (shape((TOK, D), BF16), shape((TOK, D), BF16)),
        [VM] * 4,
        flops=1 << 22,
        bytes_accessed=1 << 20,
    )(own, recv, norm_gain[None], norm_bias[None])
    blocks = [block]
    up = down = block
    for _ in range(3):
        up, down = chip_shift(up, 1), chip_shift(down, -1)
        blocks += [up, down]
    blocks.append(chip_shift(up, 1))
    stats = pl.pallas_call(
        project_kernel,
        out_shape=shape((16, 128), F32),
        grid=(4,),
        in_specs=[SM, SM, SM]
        + [pl.BlockSpec((D, 256), lambda c: (c, 0))] * 2
        + [pl.BlockSpec((TOK, D), lambda c: (0, 0))] * CHIPS,
        out_specs=pl.BlockSpec((16, 128), lambda c: (0, 0)),
        scratch_shapes=[pltpu.VMEM((128, 512), F32)],
        cost_estimate=pl.CostEstimate(
            flops=1 << 29, bytes_accessed=7 << 20, transcendentals=0
        ),
    )(me1, grid, owner, merge_weight, merge_other, *blocks)
    stats = lax.all_to_all(stats, "seq", split_axis=0, concat_axis=0, tiled=True)
    final = call(final_kernel, shape((8, 128), F32), [SM, SM, SM, VM])(
        me1, grid, owner, stats
    )
    return (normed[None], final[0:1, 0:1], final[0:1, 1:2])


def solution(mesh):
    placed = (
        P("rows", "seq", None),
        P("rows", "seq", None),
        P("rows", "seq"),
        P("rows", "seq"),
        P("rows", None, None),
        P("rows", None),
        P("rows", None),
        P(),
        P(),
        P(None, "seq"),
    )
    return jax.shard_map(
        body,
        mesh=mesh,
        in_specs=placed,
        out_specs=(P("rows", "seq", None), P("rows", "seq"), P("rows", "seq")),
        check_vma=False,
    )
```

```python
import jax
import jax.numpy as jnp
import numpy as np
from jax import lax
from jax.experimental import pallas as pl
from jax.experimental.pallas import tpu as pltpu
from jax.sharding import PartitionSpec as P


D = 1280
HEADS = 16
HD = 80
OUT = 4096
IMGS = 4
SEQ = 1024
TOK = 64
CHIPS = 8
MAXIMG = 896
NEG = -1e30


F32 = jnp.float32
BF16 = jnp.bfloat16
VM = pl.BlockSpec(memory_space=pltpu.VMEM)
SM = pl.BlockSpec(memory_space=pltpu.SMEM)


def iota(shape, dim):
    return lax.broadcasted_iota(jnp.int32, shape, dim)


def image_bounds(grid_ref):
    starts, ends, total = [], [], 0
    for j in range(IMGS):
        starts.append(total)
        total = total + grid_ref[0, j, 0] * grid_ref[0, j, 1]
        ends.append(total)
    return starts, ends


def rotary_kernel(grid_ref, keep_ref, qkv_ref, out_ref):
    starts, ends = image_bounds(grid_ref)
    place = lax.axis_index("seq") * TOK + iota((TOK, 256), 0)
    begin = jnp.zeros((TOK, 256), jnp.int32)
    width = jnp.full((TOK, 256), 2, jnp.int32)
    for j in range(IMGS):
        inside = (place >= starts[j]) & (place < ends[j])
        begin = jnp.where(inside, starts[j], begin)
        width = jnp.where(inside, grid_ref[0, j, 1], width)
    valid = place < ends[IMGS - 1]
    offset = place - begin
    square = lax.shift_right_logical(offset, 2)
    corner = offset & 3
    half = lax.shift_right_logical(width, 1)
    line = jnp.floor((square.astype(F32) + 0.5) / half.astype(F32)).astype(jnp.int32)
    row = 2 * line + lax.shift_right_logical(corner, 1)
    col = 2 * (square - line * half) + (corner & 1)
    row = jnp.where(valid, row, 0).astype(F32)
    col = jnp.where(valid, col, 0).astype(F32)
    lane = iota((TOK, 256), 1) & 127
    rotated = lane < HD
    pair = lane
    for _ in range(5):
        pair = jnp.where(pair >= 20, pair - 20, pair)
    rate = jnp.exp(pair.astype(F32) * (-np.log(10000.0) / 20))
    angle = jnp.where(lane < HD // 2, row, col) * rate
    cosine = jnp.where(rotated, jnp.cos(angle), 1.0)
    low = (lane < 20) | ((lane >= 40) & (lane < 60))
    sine = jnp.sin(angle)
    sine = jnp.where(rotated, jnp.where(low, -sine, sine), 0.0)
    diagonal = iota((TOK, TOK), 0) == iota((TOK, TOK), 1)
    flags = jnp.where(diagonal, keep_ref[...].astype(F32), 0.0)
    tail = jnp.broadcast_to(jnp.sum(flags, axis=1, keepdims=True), (TOK, 16))
    for dest in range(HEADS):
        q = qkv_ref[0, :, dest * HD : dest * HD + HD].astype(F32)
        k = qkv_ref[0, :, D + dest * HD : D + dest * HD + HD].astype(F32)
        v = qkv_ref[0, :, 2 * D + dest * HD : 2 * D + dest * HD + HD].astype(F32)
        full = jnp.concatenate([q, v[:, :48], k, v[:, 48:], tail], axis=1)
        swapped = jnp.where(low, pltpu.roll(full, 256 - 20, 1), pltpu.roll(full, 20, 1))
        out_ref[dest] = (full * cosine + swapped * sine).astype(BF16)


def attention_kernel(grid_ref, x_ref, out_ref):
    starts, ends = image_bounds(grid_ref)
    pick = jnp.where(iota((8, 128), 1) == 112, 1.0, 0.0).astype(BF16)
    keep = lax.dot_general(
        pick, x_ref[:, 128:], (((1,), (1,)), ((), ())), preferred_element_type=F32
    )[0:1]
    key_place = jnp.where(keep > 0.5, iota((1, SEQ), 1), -1)
    query_lane = iota((128, 128), 1) < HD

    def emit(chip, rows):
        flipped = jnp.transpose(rows)
        out_ref[chip] = jnp.concatenate(
            [flipped[80:128], flipped[208:240]], axis=0
        ).astype(BF16)

    for chip in range(MAXIMG // 128):
        first = chip * 128
        low = max(0, first - 256)
        high = min(MAXIMG, first + 384)
        query = jnp.where(query_lane, x_ref[first : first + 128, 0:128], 0)
        scores = lax.dot_general(
            query,
            x_ref[low:high, 128:256],
            (((1,), (1,)), ((), ())),
            preferred_element_type=F32,
        ) * HD ** (-0.5)
        place = first + iota((128, 1), 0)
        lo = place
        hi = place
        for j in range(IMGS):
            inside = (place >= starts[j]) & (place < ends[j])
            lo = jnp.where(inside, starts[j], lo)
            hi = jnp.where(inside, ends[j], hi)
        keys = key_place[:, low:high]
        same = (keys >= lo) & (keys < hi)
        own = iota((1, high - low), 1) + low == place
        scores = jnp.where(same | own, scores, NEG)
        top = jnp.max(scores, axis=1, keepdims=True)
        weights = jnp.exp(scores - top)
        total = jnp.sum(weights, axis=1, keepdims=True)
        summed = jnp.dot(
            weights.astype(BF16), x_ref[low:high, :], preferred_element_type=F32
        )
        emit(chip, summed / total)
    emit(CHIPS - 1, x_ref[MAXIMG:SEQ, :].astype(F32))


def mix_kernel(heads_ref, weight_ref, hidden_ref, own_ref, send_ref, part_ref):
    part_ref[...] = lax.dot_general(
        heads_ref[...],
        weight_ref[...],
        (((0,), (0,)), ((), ())),
        preferred_element_type=F32,
    )
    core = lax.axis_index("seq") & 1
    mine = pl.multiple_of(core * TOK, TOK)
    other = pl.multiple_of((1 - core) * TOK, TOK)
    own_ref[...] = part_ref[pl.ds(mine, TOK), :] + hidden_ref[0].astype(F32)
    send_ref[...] = part_ref[pl.ds(other, TOK), :]


def norm_kernel(own_ref, recv_ref, gain_ref, bias_ref, normed_ref, block_ref):
    mixed = own_ref[...] + recv_ref[...]
    centred = mixed - jnp.mean(mixed, axis=1, keepdims=True)
    spread = jnp.mean(centred * centred, axis=1, keepdims=True)
    normed = centred * lax.rsqrt(spread + 1e-05) * gain_ref[...].reshape(1, D) + bias_ref[...].reshape(1, D)
    normed = normed.astype(BF16)
    normed_ref[0] = normed
    line = iota((TOK, TOK), 0)
    source = 4 * (line & 15) + lax.shift_right_logical(line, 4)
    order = jnp.where(iota((TOK, TOK), 1) == source, 1.0, 0.0).astype(BF16)
    block = jnp.dot(order, normed, preferred_element_type=F32).astype(BF16)
    for chip in range(CHIPS):
        block_ref[chip] = block


def project_kernel(grid_ref, owner_ref, wa_ref, wb_ref, blocks_ref, out_ref):
    halves = []
    for w_ref in (wa_ref, wb_ref):
        part = 0.0
        for corner in range(4):
            rows = jnp.concatenate(
                [blocks_ref[c, 16 * corner : 16 * corner + 16, :] for c in range(CHIPS)],
                axis=0,
            )
            part = part + jnp.dot(
                rows, w_ref[D * corner : D * corner + D, :], preferred_element_type=F32
            )
        halves.append(part)
    done = jnp.concatenate(halves, axis=1)
    squares = jnp.sum(done * done, axis=1, keepdims=True)
    peaks = jnp.max(done, axis=1, keepdims=True)
    _, ends = image_bounds(grid_ref)
    line = iota((128, 128), 0)
    source = 2 * lax.shift_right_logical(line, 4) + (lax.axis_index("seq") & 1)
    token = source * TOK + 4 * (line & 15)
    slot = jnp.full((128, 128), -1, jnp.int32)
    for j in reversed(range(IMGS)):
        slot = jnp.where(token < ends[j], owner_ref[0, j], slot)
    hot = slot == iota((128, 128), 1)
    sums = jnp.sum(jnp.where(hot, squares, 0.0), axis=0, keepdims=True)
    tops = jnp.max(jnp.where(hot, peaks, NEG), axis=0, keepdims=True)
    both = jnp.where(line == 0, sums, jnp.where(line == 1, tops, 0.0))
    out_ref[...] = jnp.transpose(both)[:16]


def final_kernel(grid_ref, owner_ref, stats_ref, norm_ref, peak_ref):
    stats = stats_ref[...]
    total = jnp.sum(stats, axis=0, keepdims=True)[:, 0:1]
    top = jnp.max(stats, axis=0, keepdims=True)[:, 1:2]
    me = lax.axis_index("seq")
    count = 0
    for j in range(IMGS):
        size = lax.shift_right_logical(grid_ref[0, j, 0] * grid_ref[0, j, 1], 2)
        count = count + jnp.where(owner_ref[0, j] == me, size, 0)
    counts = jnp.full((1, 1), count, jnp.int32)
    divisor = (jnp.maximum(counts, 1) * OUT).astype(F32)
    norm_ref[...] = jnp.where(counts > 0, jnp.sqrt(total / divisor + 1e-06), 0.0)
    peak_ref[...] = jnp.where(counts > 0, top, 0.0)


def call(kernel, out, specs, scratch=(), flops=0, bytes_accessed=0, mib=8):
    many = isinstance(out, (tuple, list))
    return pl.pallas_call(
        kernel,
        out_shape=out,
        in_specs=specs,
        out_specs=tuple([VM] * len(out)) if many else VM,
        scratch_shapes=scratch,
        cost_estimate=pl.CostEstimate(
            flops=flops, bytes_accessed=bytes_accessed, transcendentals=0
        ),
        compiler_params=pltpu.CompilerParams(vmem_limit_bytes=mib << 20),
    )


def shape(dims, dtype):
    return jax.ShapeDtypeStruct(dims, dtype)


def chip_shift(x, step, flip=0):
    pairs = []
    for s in range(2 * CHIPS):
        chip, core = s // 2, s % 2
        pairs.append((s, ((chip + step) % CHIPS) * 2 + (core ^ flip)))
    return lax.ppermute(x, "seq", pairs)


def gather_weight(weight):
    groups = [[z * 4 + x for z in range(8)] for x in range(4)]
    column = lax.all_to_all(
        jnp.broadcast_to(weight[None], (8, 40, D)),
        "rows",
        split_axis=0,
        concat_axis=0,
        axis_index_groups=groups,
        tiled=True,
    )

    def shift_x(step, cores):
        pairs = []
        for r in range(32):
            z, x = r // 4, r % 4
            for s in range(16):
                if (x - 2 * (s % 2)) % 4 in cores:
                    pairs.append((r * 16 + s, (z * 4 + (x + step) % 4) * 16 + s))
        return lax.ppermute(column, ("rows", "seq"), pairs)

    two = shift_x(2, (0, 1))
    plus = shift_x(1, (0, 1))
    minus = shift_x(-1, (0, 1))
    rel = (lax.axis_index("rows") - 2 * (lax.axis_index("seq") % 2)) % 4

    def pick(a, b, c, d):
        return jnp.where(
            rel == 0, a, jnp.where(rel == 1, b, jnp.where(rel == 2, c, d))
        )

    pair = jnp.concatenate(
        [pick(column, plus, two, minus), pick(minus, column, plus, two)], axis=1
    )
    return pair.reshape(640, D)


def body(
    qkv,
    hidden,
    segment_ids,
    key_keep,
    grid_sizes,
    owner_slots,
    out_weight,
    norm_gain,
    norm_bias,
    merge_weight,
):
    del segment_ids
    weight = gather_weight(out_weight)
    packed = call(
        rotary_kernel,
        shape((HEADS, TOK, 256), BF16),
        [SM, VM, VM],
        flops=1 << 22,
        bytes_accessed=1 << 20,
    )(grid_sizes, key_keep, qkv)
    heads_all = lax.all_to_all(packed, "seq", split_axis=0, concat_axis=0, tiled=True)
    merge_other = chip_shift(merge_weight, 0, 1)
    head_out = call(
        attention_kernel,
        shape((CHIPS, HD, 128), BF16),
        [SM, VM],
        flops=1 << 29,
        bytes_accessed=1 << 20,
    )(grid_sizes, heads_all.reshape(SEQ, 256))
    groups = [[2 * c + p for c in range(CHIPS)] for p in range(2)]
    attended = lax.all_to_all(
        head_out,
        "seq",
        split_axis=0,
        concat_axis=0,
        axis_index_groups=groups,
        tiled=True,
    ).reshape(640, 128)
    own, send = call(
        mix_kernel,
        (shape((TOK, D), F32), shape((TOK, D), F32)),
        [VM, VM, VM],
        scratch=[pltpu.VMEM((128, D), F32)],
        flops=1 << 28,
        bytes_accessed=3 << 20,
    )(attended, weight, hidden)
    recv = chip_shift(send, 0, 1)
    normed, blocks = call(
        norm_kernel,
        (shape((1, TOK, D), BF16), shape((CHIPS, TOK, D), BF16)),
        [VM] * 4,
        flops=1 << 22,
        bytes_accessed=1 << 20,
    )(own, recv, norm_gain, norm_bias)
    blocks = lax.all_to_all(
        blocks,
        "seq",
        split_axis=0,
        concat_axis=0,
        axis_index_groups=groups,
        tiled=True,
    )
    stats = call(
        project_kernel,
        shape((16, 128), F32),
        [SM, SM, VM, VM, VM],
        flops=1 << 29,
        bytes_accessed=7 << 20,
        mib=16,
    )(grid_sizes, owner_slots, merge_weight, merge_other, blocks)
    stats = lax.all_to_all(stats, "seq", split_axis=0, concat_axis=0, tiled=True)
    norm, peak = call(
        final_kernel, (shape((1, 1), F32), shape((1, 1), F32)), [SM, SM, VM]
    )(grid_sizes, owner_slots, stats)
    return (normed, norm, peak)


def solution(mesh):
    placed = (
        P("rows", "seq", None),
        P("rows", "seq", None),
        P("rows", "seq"),
        P("rows", "seq"),
        P("rows", None, None),
        P("rows", None),
        P("rows", None),
        P(),
        P(),
        P(None, "seq"),
    )

    return jax.shard_map(
        body,
        mesh=mesh,
        in_specs=placed,
        out_specs=(P("rows", "seq", None), P("rows", "seq"), P("rows", "seq")),
        check_vma=False,
    )
```

```python
import jax
import jax.numpy as jnp
import numpy as np
from jax import lax
from jax.experimental import pallas as pl
from jax.experimental.pallas import tpu as pltpu
from jax.sharding import PartitionSpec as P


D = 1280
HEADS = 16
HD = 80
OUT = 4096
IMGS = 4
SEQ = 1024
TOK = 64
CHIPS = 8
MAXIMG = 896
NEG = -1e30


F32 = jnp.float32
BF16 = jnp.bfloat16
VM = pl.BlockSpec(memory_space=pltpu.VMEM)
SM = pl.BlockSpec(memory_space=pltpu.SMEM)


def iota(shape, dim):
    return lax.broadcasted_iota(jnp.int32, shape, dim)


def image_bounds(grid_ref):
    starts, ends, total = [], [], 0
    for j in range(IMGS):
        starts.append(total)
        total = total + grid_ref[0, j, 0] * grid_ref[0, j, 1]
        ends.append(total)
    return starts, ends


def rotary_kernel(grid_ref, keep_ref, qkv_ref, out_ref):
    starts, ends = image_bounds(grid_ref)
    place = lax.axis_index("seq") * TOK + iota((TOK, 256), 0)
    begin = jnp.zeros((TOK, 256), jnp.int32)
    width = jnp.full((TOK, 256), 2, jnp.int32)
    for j in range(IMGS):
        inside = (place >= starts[j]) & (place < ends[j])
        begin = jnp.where(inside, starts[j], begin)
        width = jnp.where(inside, grid_ref[0, j, 1], width)
    valid = place < ends[IMGS - 1]
    offset = place - begin
    square = lax.shift_right_logical(offset, 2)
    corner = offset & 3
    half = lax.shift_right_logical(width, 1)
    line = jnp.floor((square.astype(F32) + 0.5) / half.astype(F32)).astype(jnp.int32)
    row = 2 * line + lax.shift_right_logical(corner, 1)
    col = 2 * (square - line * half) + (corner & 1)
    row = jnp.where(valid, row, 0).astype(F32)
    col = jnp.where(valid, col, 0).astype(F32)
    lane = iota((TOK, 256), 1) & 127
    rotated = lane < HD
    pair = lane
    for _ in range(5):
        pair = jnp.where(pair >= 20, pair - 20, pair)
    rate = jnp.exp(pair.astype(F32) * (-np.log(10000.0) / 20))
    angle = jnp.where(lane < HD // 2, row, col) * rate
    cosine = jnp.where(rotated, jnp.cos(angle), 1.0)
    low = (lane < 20) | ((lane >= 40) & (lane < 60))
    sine = jnp.sin(angle)
    sine = jnp.where(rotated, jnp.where(low, -sine, sine), 0.0)
    diagonal = iota((TOK, TOK), 0) == iota((TOK, TOK), 1)
    flags = jnp.where(diagonal, keep_ref[...].astype(F32), 0.0)
    tail = jnp.broadcast_to(jnp.sum(flags, axis=1, keepdims=True), (TOK, 16))
    for dest in range(HEADS):
        q = qkv_ref[0, :, dest * HD : dest * HD + HD].astype(F32)
        k = qkv_ref[0, :, D + dest * HD : D + dest * HD + HD].astype(F32)
        v = qkv_ref[0, :, 2 * D + dest * HD : 2 * D + dest * HD + HD].astype(F32)
        full = jnp.concatenate([q, v[:, :48], k, v[:, 48:], tail], axis=1)
        swapped = jnp.where(low, pltpu.roll(full, 256 - 20, 1), pltpu.roll(full, 20, 1))
        out_ref[dest] = (full * cosine + swapped * sine).astype(BF16)


def attention_kernel(grid_ref, x_ref, out_ref):
    starts, ends = image_bounds(grid_ref)
    pick = jnp.where(iota((8, 128), 1) == 112, 1.0, 0.0).astype(BF16)
    keep = lax.dot_general(
        pick, x_ref[:, 128:], (((1,), (1,)), ((), ())), preferred_element_type=F32
    )[0:1]
    key_place = jnp.where(keep > 0.5, iota((1, SEQ), 1), -1)
    query_lane = iota((128, 128), 1) < HD

    def emit(chip, rows):
        flipped = jnp.transpose(rows)
        out_ref[chip] = jnp.concatenate(
            [flipped[80:128], flipped[208:240]], axis=0
        ).astype(BF16)

    for chip in range(MAXIMG // 128):
        first = chip * 128
        low = max(0, first - 256)
        high = min(MAXIMG, first + 384)
        query = jnp.where(query_lane, x_ref[first : first + 128, 0:128], 0)
        scores = lax.dot_general(
            query,
            x_ref[low:high, 128:256],
            (((1,), (1,)), ((), ())),
            preferred_element_type=F32,
        ) * HD ** (-0.5)
        place = first + iota((128, 1), 0)
        lo = place
        hi = place
        for j in range(IMGS):
            inside = (place >= starts[j]) & (place < ends[j])
            lo = jnp.where(inside, starts[j], lo)
            hi = jnp.where(inside, ends[j], hi)
        keys = key_place[:, low:high]
        same = (keys >= lo) & (keys < hi)
        own = iota((1, high - low), 1) + low == place
        scores = jnp.where(same | own, scores, NEG)
        top = jnp.max(scores, axis=1, keepdims=True)
        weights = jnp.exp(scores - top)
        total = jnp.sum(weights, axis=1, keepdims=True)
        summed = jnp.dot(
            weights.astype(BF16), x_ref[low:high, :], preferred_element_type=F32
        )
        emit(chip, summed / total)
    emit(CHIPS - 1, x_ref[MAXIMG:SEQ, :].astype(F32))


RING = (0, -1, 1, -2, 2, -3, 3, -4)


def mix_kernel(heads_ref, hidden_ref, *refs):
    own_ref, send_ref, part_ref = refs[CHIPS:]
    z = lax.shift_right_logical(lax.axis_index("rows"), 2)
    heads = jnp.concatenate([heads_ref[(z + step) & 7] for step in RING], axis=0)
    weight = jnp.concatenate([ref[...] for ref in refs[:CHIPS]], axis=0)
    part_ref[...] = lax.dot_general(
        heads, weight, (((0,), (0,)), ((), ())), preferred_element_type=F32
    )
    core = lax.axis_index("seq") & 1
    mine = pl.multiple_of(core * TOK, TOK)
    other = pl.multiple_of((1 - core) * TOK, TOK)
    own_ref[...] = part_ref[pl.ds(mine, TOK), :] + hidden_ref[0].astype(F32)
    send_ref[...] = part_ref[pl.ds(other, TOK), :]


def norm_kernel(own_ref, recv_ref, gain_ref, bias_ref, normed_ref, block_ref):
    mixed = own_ref[...] + recv_ref[...]
    centred = mixed - jnp.mean(mixed, axis=1, keepdims=True)
    spread = jnp.mean(centred * centred, axis=1, keepdims=True)
    normed = centred * lax.rsqrt(spread + 1e-05) * gain_ref[...].reshape(1, D) + bias_ref[...].reshape(1, D)
    normed = normed.astype(BF16)
    normed_ref[0] = normed
    line = iota((TOK, TOK), 0)
    source = 4 * (line & 15) + lax.shift_right_logical(line, 4)
    order = jnp.where(iota((TOK, TOK), 1) == source, 1.0, 0.0).astype(BF16)
    block = jnp.dot(order, normed, preferred_element_type=F32).astype(BF16)
    for chip in range(CHIPS):
        block_ref[chip] = block


def project_kernel(grid_ref, owner_ref, wa_ref, wb_ref, blocks_ref, out_ref):
    halves = []
    for w_ref in (wa_ref, wb_ref):
        part = 0.0
        for corner in range(4):
            rows = jnp.concatenate(
                [blocks_ref[c, 16 * corner : 16 * corner + 16, :] for c in range(CHIPS)],
                axis=0,
            )
            part = part + jnp.dot(
                rows, w_ref[D * corner : D * corner + D, :], preferred_element_type=F32
            )
        halves.append(part)
    done = jnp.concatenate(halves, axis=1)
    squares = jnp.sum(done * done, axis=1, keepdims=True)
    peaks = jnp.max(done, axis=1, keepdims=True)
    _, ends = image_bounds(grid_ref)
    line = iota((128, 128), 0)
    source = 2 * lax.shift_right_logical(line, 4) + (lax.axis_index("seq") & 1)
    token = source * TOK + 4 * (line & 15)
    slot = jnp.full((128, 128), -1, jnp.int32)
    for j in reversed(range(IMGS)):
        slot = jnp.where(token < ends[j], owner_ref[0, j], slot)
    hot = slot == iota((128, 128), 1)
    sums = jnp.sum(jnp.where(hot, squares, 0.0), axis=0, keepdims=True)
    tops = jnp.max(jnp.where(hot, peaks, NEG), axis=0, keepdims=True)
    both = jnp.where(line == 0, sums, jnp.where(line == 1, tops, 0.0))
    out_ref[...] = jnp.transpose(both)[:16]


def final_kernel(grid_ref, owner_ref, stats_ref, norm_ref, peak_ref):
    stats = stats_ref[...]
    total = jnp.sum(stats, axis=0, keepdims=True)[:, 0:1]
    top = jnp.max(stats, axis=0, keepdims=True)[:, 1:2]
    me = lax.axis_index("seq")
    count = 0
    for j in range(IMGS):
        size = lax.shift_right_logical(grid_ref[0, j, 0] * grid_ref[0, j, 1], 2)
        count = count + jnp.where(owner_ref[0, j] == me, size, 0)
    counts = jnp.full((1, 1), count, jnp.int32)
    divisor = (jnp.maximum(counts, 1) * OUT).astype(F32)
    norm_ref[...] = jnp.where(counts > 0, jnp.sqrt(total / divisor + 1e-06), 0.0)
    peak_ref[...] = jnp.where(counts > 0, top, 0.0)


def call(kernel, out, specs, scratch=(), flops=0, bytes_accessed=0, mib=8):
    many = isinstance(out, (tuple, list))
    return pl.pallas_call(
        kernel,
        out_shape=out,
        in_specs=specs,
        out_specs=tuple([VM] * len(out)) if many else VM,
        scratch_shapes=scratch,
        cost_estimate=pl.CostEstimate(
            flops=flops, bytes_accessed=bytes_accessed, transcendentals=0
        ),
        compiler_params=pltpu.CompilerParams(vmem_limit_bytes=mib << 20),
    )


def shape(dims, dtype):
    return jax.ShapeDtypeStruct(dims, dtype)


def chip_shift(x, step, flip=0):
    pairs = []
    for s in range(2 * CHIPS):
        chip, core = s // 2, s % 2
        pairs.append((s, ((chip + step) % CHIPS) * 2 + (core ^ flip)))
    return lax.ppermute(x, "seq", pairs)


def gather_weight(weight):
    def shift_x(step):
        pairs = []
        for r in range(32):
            z, x = r // 4, r % 4
            for s in range(16):
                if (x - 2 * (s % 2)) % 4 < 2:
                    pairs.append((r * 16 + s, (z * 4 + (x + step) % 4) * 16 + s))
        return lax.ppermute(weight, ("rows", "seq"), pairs)

    def shift_z(value, step):
        pairs = [(r, (r + 4 * step) % 32) for r in range(32)]
        return lax.ppermute(value, "rows", pairs)

    two, plus, minus = shift_x(2), shift_x(1), shift_x(-1)
    rel = (lax.axis_index("rows") - 2 * (lax.axis_index("seq") & 1)) & 3

    def pick(a, b, c, d):
        return jnp.where(
            rel == 0, a, jnp.where(rel == 1, b, jnp.where(rel == 2, c, d))
        )

    pair = jnp.concatenate(
        [pick(weight, plus, two, minus), pick(minus, weight, plus, two)], axis=0
    )
    blocks = [pair]
    up = down = pair
    for _ in range(1, 4):
        up = shift_z(up, 1)
        down = shift_z(down, -1)
        blocks += [up, down]
    blocks.append(shift_z(up, 1))
    return blocks


def body(
    qkv,
    hidden,
    segment_ids,
    key_keep,
    grid_sizes,
    owner_slots,
    out_weight,
    norm_gain,
    norm_bias,
    merge_weight,
):
    del segment_ids
    weight = gather_weight(out_weight)
    packed = call(
        rotary_kernel,
        shape((HEADS, TOK, 256), BF16),
        [SM, VM, VM],
        flops=1 << 22,
        bytes_accessed=1 << 20,
    )(grid_sizes, key_keep, qkv)
    heads_all = lax.all_to_all(packed, "seq", split_axis=0, concat_axis=0, tiled=True)
    merge_other = chip_shift(merge_weight, 0, 1)
    head_out = call(
        attention_kernel,
        shape((CHIPS, HD, 128), BF16),
        [SM, VM],
        flops=1 << 29,
        bytes_accessed=1 << 20,
    )(grid_sizes, heads_all.reshape(SEQ, 256))
    groups = [[2 * c + p for c in range(CHIPS)] for p in range(2)]
    attended = lax.all_to_all(
        head_out,
        "seq",
        split_axis=0,
        concat_axis=0,
        axis_index_groups=groups,
        tiled=True,
    )
    own, send = call(
        mix_kernel,
        (shape((TOK, D), F32), shape((TOK, D), F32)),
        [VM] * (2 + CHIPS),
        scratch=[pltpu.VMEM((128, D), F32)],
        flops=1 << 28,
        bytes_accessed=3 << 20,
    )(attended, hidden, *weight)
    recv = chip_shift(send, 0, 1)
    normed, blocks = call(
        norm_kernel,
        (shape((1, TOK, D), BF16), shape((CHIPS, TOK, D), BF16)),
        [VM] * 4,
        flops=1 << 22,
        bytes_accessed=1 << 20,
    )(own, recv, norm_gain, norm_bias)
    blocks, merge_other = lax.optimization_barrier((blocks, merge_other))
    blocks = lax.all_to_all(
        blocks,
        "seq",
        split_axis=0,
        concat_axis=0,
        axis_index_groups=groups,
        tiled=True,
    )
    stats = call(
        project_kernel,
        shape((16, 128), F32),
        [SM, SM, VM, VM, VM],
        flops=1 << 29,
        bytes_accessed=7 << 20,
        mib=16,
    )(grid_sizes, owner_slots, merge_weight, merge_other, blocks)
    stats = lax.all_to_all(stats, "seq", split_axis=0, concat_axis=0, tiled=True)
    norm, peak = call(
        final_kernel, (shape((1, 1), F32), shape((1, 1), F32)), [SM, SM, VM]
    )(grid_sizes, owner_slots, stats)
    return (normed, norm, peak)


def solution(mesh):
    placed = (
        P("rows", "seq", None),
        P("rows", "seq", None),
        P("rows", "seq"),
        P("rows", "seq"),
        P("rows", None, None),
        P("rows", None),
        P("rows", None),
        P(),
        P(),
        P(None, "seq"),
    )

    return jax.shard_map(
        body,
        mesh=mesh,
        in_specs=placed,
        out_specs=(P("rows", "seq", None), P("rows", "seq"), P("rows", "seq")),
        check_vma=False,
    )
```

```python
import jax
import jax.numpy as jnp
import numpy as np
from jax import lax
from jax.experimental import pallas as pl
from jax.experimental.pallas import tpu as pltpu
from jax.sharding import PartitionSpec as P


D = 1280
HEADS = 16
HD = 80
OUT = 4096
IMGS = 4
SEQ = 1024
TOK = 64
CHIPS = 8
MAXIMG = 896
NEG = -1e30


F32 = jnp.float32
BF16 = jnp.bfloat16
VM = pl.BlockSpec(memory_space=pltpu.VMEM)
SM = pl.BlockSpec(memory_space=pltpu.SMEM)


def iota(shape, dim):
    return lax.broadcasted_iota(jnp.int32, shape, dim)


def image_bounds(grid_ref):
    starts, ends, total = [], [], 0
    for j in range(IMGS):
        starts.append(total)
        total = total + grid_ref[0, 0, j] * grid_ref[0, 1, j]
        ends.append(total)
    return starts, ends


def rotary_kernel(grid_ref, keep_ref, qkv_ref, out_ref):
    starts, ends = image_bounds(grid_ref)
    place = lax.axis_index("seq") * TOK + iota((TOK, 256), 0)
    begin = jnp.zeros((TOK, 256), jnp.int32)
    width = jnp.full((TOK, 256), 2, jnp.int32)
    for j in range(IMGS):
        inside = (place >= starts[j]) & (place < ends[j])
        begin = jnp.where(inside, starts[j], begin)
        width = jnp.where(inside, grid_ref[0, 1, j], width)
    valid = place < ends[IMGS - 1]
    offset = place - begin
    square = lax.shift_right_logical(offset, 2)
    corner = offset & 3
    half = lax.shift_right_logical(width, 1)
    line = jnp.floor((square.astype(F32) + 0.5) / half.astype(F32)).astype(jnp.int32)
    row = 2 * line + lax.shift_right_logical(corner, 1)
    col = 2 * (square - line * half) + (corner & 1)
    row = jnp.where(valid, row, 0).astype(F32)
    col = jnp.where(valid, col, 0).astype(F32)
    lane = iota((TOK, 256), 1) & 127
    rotated = lane < HD
    pair = lane
    for _ in range(5):
        pair = jnp.where(pair >= 20, pair - 20, pair)
    rate = jnp.exp(pair.astype(F32) * (-np.log(10000.0) / 20))
    angle = jnp.where(lane < HD // 2, row, col) * rate
    cosine = jnp.where(rotated, jnp.cos(angle), 1.0)
    low = (lane < 20) | ((lane >= 40) & (lane < 60))
    sine = jnp.sin(angle)
    sine = jnp.where(rotated, jnp.where(low, -sine, sine), 0.0)
    diagonal = iota((TOK, TOK), 0) == iota((TOK, TOK), 1)
    flags = jnp.where(diagonal, keep_ref[...].astype(F32), 0.0)
    tail = jnp.broadcast_to(jnp.sum(flags, axis=1, keepdims=True), (TOK, 16))
    z = lax.shift_right_logical(lax.axis_index("rows"), 2)
    for head in range(HEADS):
        behind = (z - head // 2) & 7
        ahead = (head // 2 - z) & 7
        low_core = (behind >= 1) & (behind <= 4)
        place = jnp.where(low_core, behind - 1, (ahead + 3) & 3) + 4 * (head % 2)
        dest = 2 * place + jnp.where(low_core, 0, 1)
        q = qkv_ref[0, :, head * HD : head * HD + HD].astype(F32)
        k = qkv_ref[0, :, D + head * HD : D + head * HD + HD].astype(F32)
        v = qkv_ref[0, :, 2 * D + head * HD : 2 * D + head * HD + HD].astype(F32)
        full = jnp.concatenate([q, v[:, :48], k, v[:, 48:], tail], axis=1)
        swapped = jnp.where(low, pltpu.roll(full, 256 - 20, 1), pltpu.roll(full, 20, 1))
        out_ref[dest] = (full * cosine + swapped * sine).astype(BF16)


def attention_kernel(grid_ref, x_ref, out_ref):
    starts, ends = image_bounds(grid_ref)
    pick = jnp.where(iota((8, 128), 1) == 112, 1.0, 0.0).astype(BF16)
    keep = lax.dot_general(
        pick, x_ref[:, 128:], (((1,), (1,)), ((), ())), preferred_element_type=F32
    )[0:1]
    key_place = jnp.where(keep > 0.5, iota((1, SEQ), 1), -1)
    query_lane = iota((128, 128), 1) < HD

    def emit(chip, rows):
        flipped = jnp.transpose(rows)
        out_ref[chip] = jnp.concatenate(
            [flipped[80:128], flipped[208:240]], axis=0
        ).astype(BF16)

    for chip in range(MAXIMG // 128):
        first = chip * 128
        low = max(0, first - 256)
        high = min(MAXIMG, first + 384)
        query = jnp.where(query_lane, x_ref[first : first + 128, 0:128], 0)
        scores = lax.dot_general(
            query,
            x_ref[low:high, 128:256],
            (((1,), (1,)), ((), ())),
            preferred_element_type=F32,
        ) * HD ** (-0.5)
        place = first + iota((128, 1), 0)
        lo = place
        hi = place
        for j in range(IMGS):
            inside = (place >= starts[j]) & (place < ends[j])
            lo = jnp.where(inside, starts[j], lo)
            hi = jnp.where(inside, ends[j], hi)
        keys = key_place[:, low:high]
        same = (keys >= lo) & (keys < hi)
        own = iota((1, high - low), 1) + low == place
        scores = jnp.where(same | own, scores, NEG)
        top = jnp.max(scores, axis=1, keepdims=True)
        weights = jnp.exp(scores - top)
        total = jnp.sum(weights, axis=1, keepdims=True)
        summed = jnp.dot(
            weights.astype(BF16), x_ref[low:high, :], preferred_element_type=F32
        )
        emit(chip, summed / total)
    emit(CHIPS - 1, x_ref[MAXIMG:SEQ, :].astype(F32))


def take_four(refs):
    core = lax.axis_index("seq") & 1
    own_ref, one, two, three, four_ref = refs
    fourth = jnp.where(core == 0, four_ref[...], own_ref[...])
    return [one[...], two[...], three[...], fourth]


def mix_kernel(heads_ref, hidden_ref, *refs):
    out_ref = refs[5]
    core = lax.axis_index("seq") & 1
    heads = jnp.concatenate(
        [heads_ref[i + 4 * half] for i in range(4) for half in range(2)], axis=0
    )
    weight = jnp.concatenate(take_four(refs[:5]), axis=0)
    out_ref[...] = lax.dot_general(
        heads, weight, (((0,), (0,)), ((), ())), preferred_element_type=F32
    )
    mine = pl.ds(pl.multiple_of(core * TOK, TOK), TOK)
    out_ref[mine, :] = out_ref[mine, :] + hidden_ref[0].astype(F32)


def norm_kernel(own_ref, recv_ref, gain_ref, bias_ref, normed_ref, block_ref, keep_ref):
    mixed = own_ref[...] + recv_ref[...]
    centred = mixed - jnp.mean(mixed, axis=1, keepdims=True)
    spread = jnp.mean(centred * centred, axis=1, keepdims=True)
    normed = centred * lax.rsqrt(spread + 1e-05) * gain_ref[...].reshape(1, D)
    normed = (normed + bias_ref[...].reshape(1, D)).astype(BF16)
    keep_ref[...] = normed
    core = lax.axis_index("seq") & 1
    normed_ref[0] = keep_ref[pl.ds(pl.multiple_of(core * TOK, TOK), TOK), :]
    line = iota((128, 128), 0)
    source = 4 * (line & 31) + lax.shift_right_logical(line, 5)
    order = jnp.where(iota((128, 128), 1) == source, 1.0, 0.0).astype(BF16)
    block_ref[...] = jnp.dot(order, normed, preferred_element_type=F32).astype(BF16)


def project_kernel(grid_ref, owner_ref, wa_ref, wb_ref, *refs):
    out_ref = refs[5]
    bundles = take_four(refs[:5])
    halves = []
    for w_ref in (wa_ref, wb_ref):
        part = 0.0
        for corner in range(4):
            rows = jnp.concatenate(
                [b[32 * corner : 32 * corner + 32, :] for b in bundles], axis=0
            )
            part = part + jnp.dot(
                rows, w_ref[D * corner : D * corner + D, :], preferred_element_type=F32
            )
        halves.append(part)
    done = jnp.concatenate(halves, axis=1)
    squares = jnp.sum(done * done, axis=1, keepdims=True)
    peaks = jnp.max(done, axis=1, keepdims=True)
    _, ends = image_bounds(grid_ref)
    line = iota((128, 128), 0)
    index = lax.axis_index("seq")
    step = lax.shift_right_logical(line, 5) + 1
    step = jnp.where((index & 1) == 0, -step, step & 3)
    source = (lax.shift_right_logical(index, 1) + step) & 7
    token = source * 128 + 4 * (line & 31)
    slot = jnp.full((128, 128), -1, jnp.int32)
    for j in reversed(range(IMGS)):
        slot = jnp.where(token < ends[j], owner_ref[0, j], slot)
    hot = slot == iota((128, 128), 1)
    sums = jnp.sum(jnp.where(hot, squares, 0.0), axis=0, keepdims=True)
    tops = jnp.max(jnp.where(hot, peaks, NEG), axis=0, keepdims=True)
    both = jnp.where(line == 0, sums, jnp.where(line == 1, tops, 0.0))
    out_ref[...] = jnp.transpose(both)[:16]


def final_kernel(grid_ref, owner_ref, stats_ref, norm_ref, peak_ref):
    stats = stats_ref[...]
    total = jnp.sum(stats, axis=0, keepdims=True)[:, 0:1]
    top = jnp.max(stats, axis=0, keepdims=True)[:, 1:2]
    me = lax.axis_index("seq")
    count = 0
    for j in range(IMGS):
        size = lax.shift_right_logical(grid_ref[0, 0, j] * grid_ref[0, 1, j], 2)
        count = count + jnp.where(owner_ref[0, j] == me, size, 0)
    counts = jnp.full((1, 1), count, jnp.int32)
    divisor = (jnp.maximum(counts, 1) * OUT).astype(F32)
    norm_ref[...] = jnp.where(counts > 0, jnp.sqrt(total / divisor + 1e-06), 0.0)
    peak_ref[...] = jnp.where(counts > 0, top, 0.0)


def call(kernel, out, specs, scratch=(), flops=0, bytes_accessed=0, mib=8):
    many = isinstance(out, (tuple, list))
    return pl.pallas_call(
        kernel,
        out_shape=out,
        in_specs=specs,
        out_specs=tuple([VM] * len(out)) if many else VM,
        scratch_shapes=scratch,
        cost_estimate=pl.CostEstimate(
            flops=flops, bytes_accessed=bytes_accessed, transcendentals=0
        ),
        compiler_params=pltpu.CompilerParams(vmem_limit_bytes=mib << 20),
    )


def shape(dims, dtype):
    return jax.ShapeDtypeStruct(dims, dtype)


def chip_shift(x, step, flip=0):
    pairs = []
    for s in range(2 * CHIPS):
        chip, core = s // 2, s % 2
        pairs.append((s, ((chip + step) % CHIPS) * 2 + (core ^ flip)))
    return lax.ppermute(x, "seq", pairs)


def two_way(axes, value, move, count):
    bundles = [value]
    for k in range(1, 5):
        pairs = []
        for index in range(count):
            core = index & 1
            if k < 4 or core == 0:
                pairs.append((index, move(index, 1 - 2 * core)))
        value = lax.ppermute(value, axes, pairs)
        bundles.append(value)
    return bundles


def gather_weight(weight):
    def shift_x(step):
        pairs = [(r, (r & ~3) + ((r + step) & 3)) for r in range(32)]
        return lax.ppermute(weight, "rows", pairs)

    two, plus, minus = shift_x(2), shift_x(1), shift_x(-1)
    here = lax.axis_index("rows") & 3
    parts = []
    for x in range(4):
        rel = (x - here) & 3
        parts.append(
            jnp.where(
                rel == 0,
                weight,
                jnp.where(rel == 1, minus, jnp.where(rel == 2, two, plus)),
            )
        )
    bundle = jnp.concatenate(parts, axis=0)

    def move(index, step):
        row, place = index // 16, index % 16
        return (row + 4 * step) % 32 * 16 + place

    return two_way(("rows", "seq"), bundle, move, 512)


def body(
    qkv,
    hidden,
    segment_ids,
    key_keep,
    grid_sizes,
    owner_slots,
    out_weight,
    norm_gain,
    norm_bias,
    merge_weight,
):
    del segment_ids
    grid_sizes = jnp.transpose(grid_sizes, (0, 2, 1))
    weight = gather_weight(out_weight)
    packed = call(
        rotary_kernel,
        shape((HEADS, TOK, 256), BF16),
        [SM, VM, VM],
        flops=1 << 22,
        bytes_accessed=1 << 20,
        mib=56,
    )(grid_sizes, key_keep, qkv)
    heads_all = lax.all_to_all(packed, "seq", split_axis=0, concat_axis=0, tiled=True)
    merge_other = chip_shift(merge_weight, 0, 1)
    head_out = call(
        attention_kernel,
        shape((CHIPS, HD, 128), BF16),
        [SM, VM],
        flops=1 << 29,
        bytes_accessed=1 << 20,
    )(grid_sizes, heads_all.reshape(SEQ, 256))
    groups = [[2 * c + p for c in range(CHIPS)] for p in range(2)]
    attended = lax.all_to_all(
        head_out,
        "seq",
        split_axis=0,
        concat_axis=0,
        axis_index_groups=groups,
        tiled=True,
    )
    mixed = call(
        mix_kernel,
        shape((128, D), F32),
        [VM] * 7,
        flops=1 << 28,
        bytes_accessed=3 << 20,
    )(attended, hidden, *weight)
    recv = chip_shift(mixed, 0, 1)
    normed, block = call(
        norm_kernel,
        (shape((1, TOK, D), BF16), shape((128, D), BF16)),
        [VM] * 4,
        scratch=[pltpu.VMEM((128, D), BF16)],
        flops=1 << 22,
        bytes_accessed=1 << 20,
    )(mixed, recv, norm_gain, norm_bias)

    def move(index, step):
        return (index + 2 * step) % 16

    bundles = two_way("seq", block, move, 16)
    stats = call(
        project_kernel,
        shape((16, 128), F32),
        [SM, SM] + [VM] * 7,
        flops=1 << 29,
        bytes_accessed=7 << 20,
        mib=16,
    )(grid_sizes, owner_slots, merge_weight, merge_other, *bundles)
    stats = lax.all_to_all(stats, "seq", split_axis=0, concat_axis=0, tiled=True)
    norm, peak = call(
        final_kernel, (shape((1, 1), F32), shape((1, 1), F32)), [SM, SM, VM]
    )(grid_sizes, owner_slots, stats)
    return (normed, norm, peak)


def solution(mesh):
    placed = (
        P("rows", "seq", None),
        P("rows", "seq", None),
        P("rows", "seq"),
        P("rows", "seq"),
        P("rows", None, None),
        P("rows", None),
        P("rows", None),
        P(),
        P(),
        P(None, "seq"),
    )

    return jax.shard_map(
        body,
        mesh=mesh,
        in_specs=placed,
        out_specs=(P("rows", "seq", None), P("rows", "seq"), P("rows", "seq")),
        check_vma=False,
    )
```

```python
import jax
import jax.numpy as jnp
import numpy as np
from jax import lax
from jax.experimental import pallas as pl
from jax.experimental.pallas import tpu as pltpu
from jax.sharding import PartitionSpec as P


D = 1280
HEADS = 16
HD = 80
OUT = 4096
IMGS = 4
SEQ = 1024
TOK = 64
CHIPS = 8
MAXIMG = 896
NEG = -1e30


F32 = jnp.float32
BF16 = jnp.bfloat16
VM = pl.BlockSpec(memory_space=pltpu.VMEM)
SM = pl.BlockSpec(memory_space=pltpu.SMEM)


def iota(shape, dim):
    return lax.broadcasted_iota(jnp.int32, shape, dim)


def image_bounds(grid_ref):
    starts, ends, total = [], [], 0
    for j in range(IMGS):
        starts.append(total)
        total = total + grid_ref[0, 0, j] * grid_ref[0, 1, j]
        ends.append(total)
    return starts, ends


def rotary_kernel(grid_ref, keep_ref, qkv_ref, out_ref):
    starts, ends = image_bounds(grid_ref)
    place = lax.axis_index("seq") * TOK + iota((TOK, 256), 0)
    begin = jnp.zeros((TOK, 256), jnp.int32)
    width = jnp.full((TOK, 256), 2, jnp.int32)
    for j in range(IMGS):
        inside = (place >= starts[j]) & (place < ends[j])
        begin = jnp.where(inside, starts[j], begin)
        width = jnp.where(inside, grid_ref[0, 1, j], width)
    valid = place < ends[IMGS - 1]
    offset = place - begin
    square = lax.shift_right_logical(offset, 2)
    corner = offset & 3
    half = lax.shift_right_logical(width, 1)
    line = jnp.floor((square.astype(F32) + 0.5) / half.astype(F32)).astype(jnp.int32)
    row = 2 * line + lax.shift_right_logical(corner, 1)
    col = 2 * (square - line * half) + (corner & 1)
    row = jnp.where(valid, row, 0).astype(F32)
    col = jnp.where(valid, col, 0).astype(F32)
    lane = iota((TOK, 256), 1) & 127
    rotated = lane < HD
    pair = lane
    for _ in range(5):
        pair = jnp.where(pair >= 20, pair - 20, pair)
    rate = jnp.exp(pair.astype(F32) * (-np.log(10000.0) / 20))
    angle = jnp.where(lane < HD // 2, row, col) * rate
    cosine = jnp.where(rotated, jnp.cos(angle), 1.0)
    low = (lane < 20) | ((lane >= 40) & (lane < 60))
    sine = jnp.sin(angle)
    sine = jnp.where(rotated, jnp.where(low, -sine, sine), 0.0)
    diagonal = iota((TOK, TOK), 0) == iota((TOK, TOK), 1)
    flags = jnp.where(diagonal, keep_ref[...].astype(F32), 0.0)
    tail = jnp.broadcast_to(jnp.sum(flags, axis=1, keepdims=True), (TOK, 16))
    z = lax.shift_right_logical(lax.axis_index("rows"), 2)
    for head in range(HEADS):
        behind = (z - head // 2) & 7
        ahead = (head // 2 - z) & 7
        low_core = (behind >= 1) & (behind <= 4)
        place = jnp.where(low_core, behind - 1, (ahead + 3) & 3) + 4 * (head % 2)
        dest = 2 * place + jnp.where(low_core, 0, 1)
        q = qkv_ref[0, :, head * HD : head * HD + HD].astype(F32)
        k = qkv_ref[0, :, D + head * HD : D + head * HD + HD].astype(F32)
        v = qkv_ref[0, :, 2 * D + head * HD : 2 * D + head * HD + HD].astype(F32)
        full = jnp.concatenate([q, v[:, :48], k, v[:, 48:], tail], axis=1)
        swapped = jnp.where(low, pltpu.roll(full, 256 - 20, 1), pltpu.roll(full, 20, 1))
        out_ref[dest] = (full * cosine + swapped * sine).astype(BF16)


def attention_kernel(grid_ref, x_ref, out_ref):
    starts, ends = image_bounds(grid_ref)
    pick = jnp.where(iota((8, 128), 1) == 112, 1.0, 0.0).astype(BF16)
    keep = lax.dot_general(
        pick, x_ref[:, 128:], (((1,), (1,)), ((), ())), preferred_element_type=F32
    )[0:1]
    key_place = jnp.where(keep > 0.5, iota((1, SEQ), 1), -1)
    query_lane = iota((128, 128), 1) < HD

    def emit(chip, rows):
        flipped = jnp.transpose(rows)
        out_ref[chip, 0] = flipped[80:120].astype(BF16)
        out_ref[chip, 1] = jnp.concatenate(
            [flipped[120:128], flipped[208:240]], axis=0
        ).astype(BF16)

    for chip in range(MAXIMG // 128):
        first = chip * 128
        low = max(0, first - 256)
        high = min(MAXIMG, first + 384)
        query = jnp.where(query_lane, x_ref[first : first + 128, 0:128], 0)
        scores = lax.dot_general(
            query,
            x_ref[low:high, 128:256],
            (((1,), (1,)), ((), ())),
            preferred_element_type=F32,
        ) * HD ** (-0.5)
        place = first + iota((128, 1), 0)
        lo = place
        hi = place
        for j in range(IMGS):
            inside = (place >= starts[j]) & (place < ends[j])
            lo = jnp.where(inside, starts[j], lo)
            hi = jnp.where(inside, ends[j], hi)
        keys = key_place[:, low:high]
        same = (keys >= lo) & (keys < hi)
        own = iota((1, high - low), 1) + low == place
        scores = jnp.where(same | own, scores, NEG)
        top = jnp.max(scores, axis=1, keepdims=True)
        weights = jnp.exp(scores - top)
        total = jnp.sum(weights, axis=1, keepdims=True)
        summed = jnp.dot(
            weights.astype(BF16), x_ref[low:high, :], preferred_element_type=F32
        )
        emit(chip, summed / total)
    emit(CHIPS - 1, x_ref[MAXIMG:SEQ, :].astype(F32))


def mix_kernel(heads_ref, hidden_ref, own_ref, plus_ref, minus_ref, two_ref, out_ref):
    core = lax.axis_index("seq") & 1
    here = lax.axis_index("rows") & 3
    heads = []
    for step in (0, -1, 1, 2):
        x = (here + step) & 3
        upper, half = lax.shift_right_logical(x, 1), x & 1
        heads += [heads_ref[i + 4 * upper, half] for i in range(4)]
    weight = [ref[...] for ref in (own_ref, plus_ref, minus_ref, two_ref)]
    out_ref[...] = lax.dot_general(
        jnp.concatenate(heads, axis=0),
        jnp.concatenate(weight, axis=0),
        (((0,), (0,)), ((), ())),
        preferred_element_type=F32,
    )
    mine = pl.ds(pl.multiple_of(core * TOK, TOK), TOK)
    out_ref[mine, :] = out_ref[mine, :] + hidden_ref[0].astype(F32)


def norm_kernel(
    own_ref, recv_ref, gain_ref, bias_ref, normed_ref, first_ref, second_ref, keep_ref
):
    mixed = own_ref[...] + recv_ref[...]
    centred = mixed - jnp.mean(mixed, axis=1, keepdims=True)
    spread = jnp.mean(centred * centred, axis=1, keepdims=True)
    normed = centred * lax.rsqrt(spread + 1e-05) * gain_ref[...].reshape(1, D)
    normed = (normed + bias_ref[...].reshape(1, D)).astype(BF16)
    keep_ref[...] = normed
    core = lax.axis_index("seq") & 1
    normed_ref[0] = keep_ref[pl.ds(pl.multiple_of(core * TOK, TOK), TOK), :]
    line = iota((128, 128), 0)
    half = (lax.shift_right_logical(line, 6) + core) & 1
    source = TOK * half + 4 * (line & 15) + (lax.shift_right_logical(line, 4) & 3)
    order = jnp.where(iota((128, 128), 1) == source, 1.0, 0.0).astype(BF16)
    chunks = jnp.dot(order, normed, preferred_element_type=F32).astype(BF16)
    first_ref[...] = chunks[:TOK]
    second_ref[...] = chunks[TOK:]


def project_kernel(grid_ref, owner_ref, wa_ref, wb_ref, *refs):
    out_ref = refs[CHIPS]
    halves = []
    for w_ref in (wa_ref, wb_ref):
        part = 0.0
        for corner in range(4):
            rows = jnp.concatenate(
                [b[16 * corner : 16 * corner + 16, :] for b in refs[:CHIPS]], axis=0
            )
            part = part + jnp.dot(
                rows, w_ref[D * corner : D * corner + D, :], preferred_element_type=F32
            )
        halves.append(part)
    done = jnp.concatenate(halves, axis=1)
    squares = jnp.sum(done * done, axis=1, keepdims=True)
    peaks = jnp.max(done, axis=1, keepdims=True)
    _, ends = image_bounds(grid_ref)
    line = iota((128, 128), 0)
    index = lax.axis_index("seq")
    core = index & 1
    chunk = lax.shift_right_logical(line, 4)
    step = lax.shift_right_logical(chunk + 1, 1)
    second = ((chunk & 1) == 0) & (chunk > 0)
    half = jnp.where(second, 1 - core, core)
    step = jnp.where(core == 0, -step, step)
    source = (lax.shift_right_logical(index, 1) + step) & 7
    token = source * 128 + half * TOK + 4 * (line & 15)
    slot = jnp.full((128, 128), -1, jnp.int32)
    for j in reversed(range(IMGS)):
        slot = jnp.where(token < ends[j], owner_ref[0, j], slot)
    hot = slot == iota((128, 128), 1)
    sums = jnp.sum(jnp.where(hot, squares, 0.0), axis=0, keepdims=True)
    tops = jnp.max(jnp.where(hot, peaks, NEG), axis=0, keepdims=True)
    both = jnp.where(line == 0, sums, jnp.where(line == 1, tops, 0.0))
    out_ref[...] = jnp.transpose(both)[:16]


def final_kernel(grid_ref, owner_ref, stats_ref, norm_ref, peak_ref):
    stats = stats_ref[...]
    total = jnp.sum(stats, axis=0, keepdims=True)[:, 0:1]
    top = jnp.max(stats, axis=0, keepdims=True)[:, 1:2]
    me = lax.axis_index("seq")
    count = 0
    for j in range(IMGS):
        size = lax.shift_right_logical(grid_ref[0, 0, j] * grid_ref[0, 1, j], 2)
        count = count + jnp.where(owner_ref[0, j] == me, size, 0)
    counts = jnp.full((1, 1), count, jnp.int32)
    divisor = (jnp.maximum(counts, 1) * OUT).astype(F32)
    norm_ref[...] = jnp.where(counts > 0, jnp.sqrt(total / divisor + 1e-06), 0.0)
    peak_ref[...] = jnp.where(counts > 0, top, 0.0)


def call(kernel, out, specs, scratch=(), flops=0, bytes_accessed=0, mib=8):
    many = isinstance(out, (tuple, list))
    return pl.pallas_call(
        kernel,
        out_shape=out,
        in_specs=specs,
        out_specs=tuple([VM] * len(out)) if many else VM,
        scratch_shapes=scratch,
        cost_estimate=pl.CostEstimate(
            flops=flops, bytes_accessed=bytes_accessed, transcendentals=0
        ),
        compiler_params=pltpu.CompilerParams(vmem_limit_bytes=mib << 20),
    )


def shape(dims, dtype):
    return jax.ShapeDtypeStruct(dims, dtype)


def chip_shift(x, step, flip=0):
    pairs = []
    for s in range(2 * CHIPS):
        chip, core = s // 2, s % 2
        pairs.append((s, ((chip + step) % CHIPS) * 2 + (core ^ flip)))
    return lax.ppermute(x, "seq", pairs)


def two_way(axes, value, move, count, cores=(0, 1)):
    pairs = []
    for index in range(count):
        core = index & 1
        if core in cores:
            pairs.append((index, move(index, 1 - 2 * core)))
    return lax.ppermute(value, axes, pairs)


def gather_weight(weight):
    def move(index, step):
        row, place = index // 16, index % 16
        return (row + 4 * step) % 32 * 16 + place

    blocks, value = [], weight
    for k in range(1, 5):
        cores = (0, 1) if k < 4 else (0,)
        value = two_way(("rows", "seq"), value, move, 512, cores)
        blocks.append(value)
    core = lax.axis_index("seq") & 1
    blocks[3] = jnp.where(core == 0, blocks[3], weight)
    bundle = jnp.concatenate(blocks, axis=0)

    def shift_x(step):
        pairs = [(r, (r & ~3) + ((r + step) & 3)) for r in range(32)]
        return lax.ppermute(bundle, "rows", pairs)

    return [bundle, shift_x(1), shift_x(-1), shift_x(2)]


def body(
    qkv,
    hidden,
    segment_ids,
    key_keep,
    grid_sizes,
    owner_slots,
    out_weight,
    norm_gain,
    norm_bias,
    merge_weight,
):
    del segment_ids
    grid_sizes = jnp.transpose(grid_sizes, (0, 2, 1))
    weight = gather_weight(out_weight)
    packed = call(
        rotary_kernel,
        shape((HEADS, TOK, 256), BF16),
        [SM, VM, VM],
        flops=1 << 22,
        bytes_accessed=1 << 20,
        mib=56,
    )(grid_sizes, key_keep, qkv)
    heads_all = lax.all_to_all(packed, "seq", split_axis=0, concat_axis=0, tiled=True)
    merge_other = chip_shift(merge_weight, 0, 1)
    head_out = call(
        attention_kernel,
        shape((CHIPS, 2, HD // 2, 128), BF16),
        [SM, VM],
        flops=1 << 29,
        bytes_accessed=1 << 20,
    )(grid_sizes, heads_all.reshape(SEQ, 256))
    groups = [[2 * c + p for c in range(CHIPS)] for p in range(2)]
    attended = lax.all_to_all(
        head_out,
        "seq",
        split_axis=0,
        concat_axis=0,
        axis_index_groups=groups,
        tiled=True,
    )
    mixed = call(
        mix_kernel,
        shape((128, D), F32),
        [VM] * 6,
        flops=1 << 28,
        bytes_accessed=3 << 20,
    )(attended, hidden, *weight)
    recv = chip_shift(mixed, 0, 1)
    normed, first, second = call(
        norm_kernel,
        (shape((1, TOK, D), BF16), shape((TOK, D), BF16), shape((TOK, D), BF16)),
        [VM] * 4,
        scratch=[pltpu.VMEM((128, D), BF16)],
        flops=1 << 22,
        bytes_accessed=1 << 20,
    )(mixed, recv, norm_gain, norm_bias)

    def move(index, step):
        return (index + 2 * step) % 16

    chunks = [first]
    for k in range(1, 5):
        first = two_way("seq", first, move, 16)
        chunks.append(first)
        if k < 4:
            second = two_way("seq", second, move, 16)
            chunks.append(second)
    stats = call(
        project_kernel,
        shape((16, 128), F32),
        [SM, SM] + [VM] * (2 + CHIPS),
        flops=1 << 29,
        bytes_accessed=7 << 20,
        mib=16,
    )(grid_sizes, owner_slots, merge_weight, merge_other, *chunks)
    stats = lax.all_to_all(stats, "seq", split_axis=0, concat_axis=0, tiled=True)
    norm, peak = call(
        final_kernel, (shape((1, 1), F32), shape((1, 1), F32)), [SM, SM, VM]
    )(grid_sizes, owner_slots, stats)
    return (normed, norm, peak)


def solution(mesh):
    placed = (
        P("rows", "seq", None),
        P("rows", "seq", None),
        P("rows", "seq"),
        P("rows", "seq"),
        P("rows", None, None),
        P("rows", None),
        P("rows", None),
        P(),
        P(),
        P(None, "seq"),
    )

    return jax.shard_map(
        body,
        mesh=mesh,
        in_specs=placed,
        out_specs=(P("rows", "seq", None), P("rows", "seq"), P("rows", "seq")),
        check_vma=False,
    )
```

```python
import jax
import jax.numpy as jnp
import numpy as np
from jax import lax
from jax.experimental import pallas as pl
from jax.experimental.pallas import tpu as pltpu
from jax.sharding import PartitionSpec as P


D = 1280
HEADS = 16
HD = 80
OUT = 4096
IMGS = 4
SEQ = 1024
TOK = 64
CHIPS = 8
MAXIMG = 896
NEG = -1e30


F32 = jnp.float32
BF16 = jnp.bfloat16
VM = pl.BlockSpec(memory_space=pltpu.VMEM)
SM = pl.BlockSpec(memory_space=pltpu.SMEM)


def iota(shape, dim):
    return lax.broadcasted_iota(jnp.int32, shape, dim)


def image_bounds(grid_ref):
    starts, ends, total = [], [], 0
    for j in range(IMGS):
        starts.append(total)
        total = total + grid_ref[0, 0, j] * grid_ref[0, 1, j]
        ends.append(total)
    return starts, ends


def rotary_kernel(grid_ref, keep_ref, qkv_ref, out_ref):
    starts, ends = image_bounds(grid_ref)
    place = lax.axis_index("seq") * TOK + iota((TOK, 256), 0)
    begin = jnp.zeros((TOK, 256), jnp.int32)
    width = jnp.full((TOK, 256), 2, jnp.int32)
    for j in range(IMGS):
        inside = (place >= starts[j]) & (place < ends[j])
        begin = jnp.where(inside, starts[j], begin)
        width = jnp.where(inside, grid_ref[0, 1, j], width)
    valid = place < ends[IMGS - 1]
    offset = place - begin
    square = lax.shift_right_logical(offset, 2)
    corner = offset & 3
    half = lax.shift_right_logical(width, 1)
    line = jnp.floor((square.astype(F32) + 0.5) / half.astype(F32)).astype(jnp.int32)
    row = 2 * line + lax.shift_right_logical(corner, 1)
    col = 2 * (square - line * half) + (corner & 1)
    row = jnp.where(valid, row, 0).astype(F32)
    col = jnp.where(valid, col, 0).astype(F32)
    lane = iota((TOK, 256), 1) & 127
    rotated = lane < HD
    pair = lane
    for _ in range(5):
        pair = jnp.where(pair >= 20, pair - 20, pair)
    rate = jnp.exp(pair.astype(F32) * (-np.log(10000.0) / 20))
    angle = jnp.where(lane < HD // 2, row, col) * rate
    cosine = jnp.where(rotated, jnp.cos(angle), 1.0)
    low = (lane < 20) | ((lane >= 40) & (lane < 60))
    sine = jnp.sin(angle)
    sine = jnp.where(rotated, jnp.where(low, -sine, sine), 0.0)
    diagonal = iota((TOK, TOK), 0) == iota((TOK, TOK), 1)
    flags = jnp.where(diagonal, keep_ref[...].astype(F32), 0.0)
    tail = jnp.broadcast_to(jnp.sum(flags, axis=1, keepdims=True), (TOK, 16))
    z = lax.shift_right_logical(lax.axis_index("rows"), 2)
    for head in range(HEADS):
        behind = (z - head // 2) & 7
        ahead = (head // 2 - z) & 7
        low_core = (behind >= 1) & (behind <= 4)
        place = jnp.where(low_core, behind - 1, (ahead + 3) & 3) + 4 * (head % 2)
        dest = 2 * place + jnp.where(low_core, 0, 1)
        q = qkv_ref[0, :, head * HD : head * HD + HD].astype(F32)
        k = qkv_ref[0, :, D + head * HD : D + head * HD + HD].astype(F32)
        v = qkv_ref[0, :, 2 * D + head * HD : 2 * D + head * HD + HD].astype(F32)
        full = jnp.concatenate([q, v[:, :48], k, v[:, 48:], tail], axis=1)
        swapped = jnp.where(low, pltpu.roll(full, 256 - 20, 1), pltpu.roll(full, 20, 1))
        out_ref[dest] = (full * cosine + swapped * sine).astype(BF16)


def attention_kernel(grid_ref, x_ref, out_ref):
    starts, ends = image_bounds(grid_ref)
    pick = jnp.where(iota((8, 128), 1) == 112, 1.0, 0.0).astype(BF16)
    keep = lax.dot_general(
        pick, x_ref[:, 128:], (((1,), (1,)), ((), ())), preferred_element_type=F32
    )[0:1]
    key_place = jnp.where(keep > 0.5, iota((1, SEQ), 1), -1)
    query_lane = iota((128, 128), 1) < HD

    def emit(chip, rows):
        flipped = jnp.transpose(rows)
        out_ref[chip, 0] = flipped[80:120].astype(BF16)
        out_ref[chip, 1] = jnp.concatenate(
            [flipped[120:128], flipped[208:240]], axis=0
        ).astype(BF16)

    for chip in range(MAXIMG // 128):
        first = chip * 128
        low = max(0, first - 256)
        high = min(MAXIMG, first + 384)
        query = jnp.where(query_lane, x_ref[first : first + 128, 0:128], 0)
        scores = lax.dot_general(
            query,
            x_ref[low:high, 128:256],
            (((1,), (1,)), ((), ())),
            preferred_element_type=F32,
        ) * HD ** (-0.5)
        place = first + iota((128, 1), 0)
        lo = place
        hi = place
        for j in range(IMGS):
            inside = (place >= starts[j]) & (place < ends[j])
            lo = jnp.where(inside, starts[j], lo)
            hi = jnp.where(inside, ends[j], hi)
        keys = key_place[:, low:high]
        same = (keys >= lo) & (keys < hi)
        own = iota((1, high - low), 1) + low == place
        scores = jnp.where(same | own, scores, NEG)
        top = jnp.max(scores, axis=1, keepdims=True)
        weights = jnp.exp(scores - top)
        total = jnp.sum(weights, axis=1, keepdims=True)
        summed = jnp.dot(
            weights.astype(BF16), x_ref[low:high, :], preferred_element_type=F32
        )
        emit(chip, summed / total)
    emit(CHIPS - 1, x_ref[MAXIMG:SEQ, :].astype(F32))


def mix_kernel(heads_ref, hidden_ref, own_ref, plus_ref, minus_ref, two_ref, out_ref):
    core = lax.axis_index("seq") & 1
    here = lax.axis_index("rows") & 3
    heads = []
    for step in (0, -1, 1, 2):
        x = (here + step) & 3
        upper, half = lax.shift_right_logical(x, 1), x & 1
        heads += [heads_ref[i + 4 * upper, half] for i in range(4)]
    weight = [ref[...] for ref in (own_ref, plus_ref, minus_ref, two_ref)]
    out_ref[...] = lax.dot_general(
        jnp.concatenate(heads, axis=0),
        jnp.concatenate(weight, axis=0),
        (((0,), (0,)), ((), ())),
        preferred_element_type=F32,
    )
    mine = pl.ds(pl.multiple_of(core * TOK, TOK), TOK)
    out_ref[mine, :] = out_ref[mine, :] + hidden_ref[0].astype(F32)


def norm_kernel(
    own_ref, recv_ref, gain_ref, bias_ref, normed_ref, first_ref, second_ref, keep_ref
):
    mixed = own_ref[...] + recv_ref[...]
    centred = mixed - jnp.mean(mixed, axis=1, keepdims=True)
    spread = jnp.mean(centred * centred, axis=1, keepdims=True)
    normed = centred * lax.rsqrt(spread + 1e-05) * gain_ref[...].reshape(1, D)
    normed = (normed + bias_ref[...].reshape(1, D)).astype(BF16)
    keep_ref[...] = normed
    core = lax.axis_index("seq") & 1
    normed_ref[0] = keep_ref[pl.ds(pl.multiple_of(core * TOK, TOK), TOK), :]
    line = iota((128, 128), 0)
    half = (lax.shift_right_logical(line, 6) + core) & 1
    source = TOK * half + 4 * (line & 15) + (lax.shift_right_logical(line, 4) & 3)
    order = jnp.where(iota((128, 128), 1) == source, 1.0, 0.0).astype(BF16)
    chunks = jnp.dot(order, normed, preferred_element_type=F32).astype(BF16)
    first_ref[...] = chunks[:TOK]
    second_ref[...] = chunks[TOK:]


def project_kernel(grid_ref, owner_ref, wa_ref, wb_ref, *refs):
    out_ref = refs[CHIPS]
    halves = []
    for w_ref in (wa_ref, wb_ref):
        part = 0.0
        for corner in range(4):
            rows = jnp.concatenate(
                [b[16 * corner : 16 * corner + 16, :] for b in refs[:CHIPS]], axis=0
            )
            part = part + jnp.dot(
                rows, w_ref[D * corner : D * corner + D, :], preferred_element_type=F32
            )
        halves.append(part)
    done = jnp.concatenate(halves, axis=1)
    squares = jnp.sum(done * done, axis=1, keepdims=True)
    peaks = jnp.max(done, axis=1, keepdims=True)
    _, ends = image_bounds(grid_ref)
    line = iota((128, 128), 0)
    index = lax.axis_index("seq")
    core = index & 1
    chunk = lax.shift_right_logical(line, 4)
    step = lax.shift_right_logical(chunk + 1, 1)
    second = ((chunk & 1) == 0) & (chunk > 0)
    half = jnp.where(second, 1 - core, core)
    step = jnp.where(core == 0, -step, step)
    source = (lax.shift_right_logical(index, 1) + step) & 7
    token = source * 128 + half * TOK + 4 * (line & 15)
    slot = jnp.full((128, 128), -1, jnp.int32)
    for j in reversed(range(IMGS)):
        slot = jnp.where(token < ends[j], owner_ref[0, j], slot)
    hot = slot == iota((128, 128), 1)
    sums = jnp.sum(jnp.where(hot, squares, 0.0), axis=0, keepdims=True)
    tops = jnp.max(jnp.where(hot, peaks, NEG), axis=0, keepdims=True)
    both = jnp.where(line == 0, sums, jnp.where(line == 1, tops, 0.0))
    out_ref[...] = jnp.transpose(both)[:16]


def final_kernel(grid_ref, owner_ref, stats_ref, norm_ref, peak_ref):
    stats = stats_ref[...]
    total = jnp.sum(stats, axis=0, keepdims=True)[:, 0:1]
    top = jnp.max(stats, axis=0, keepdims=True)[:, 1:2]
    me = lax.axis_index("seq")
    count = 0
    for j in range(IMGS):
        size = lax.shift_right_logical(grid_ref[0, 0, j] * grid_ref[0, 1, j], 2)
        count = count + jnp.where(owner_ref[0, j] == me, size, 0)
    counts = jnp.full((1, 1), count, jnp.int32)
    divisor = (jnp.maximum(counts, 1) * OUT).astype(F32)
    norm_ref[...] = jnp.where(counts > 0, jnp.sqrt(total / divisor + 1e-06), 0.0)
    peak_ref[...] = jnp.where(counts > 0, top, 0.0)


def call(kernel, out, specs, scratch=(), flops=0, bytes_accessed=0, mib=8):
    many = isinstance(out, (tuple, list))
    return pl.pallas_call(
        kernel,
        out_shape=out,
        in_specs=specs,
        out_specs=tuple([VM] * len(out)) if many else VM,
        scratch_shapes=scratch,
        cost_estimate=pl.CostEstimate(
            flops=flops, bytes_accessed=bytes_accessed, transcendentals=0
        ),
        compiler_params=pltpu.CompilerParams(vmem_limit_bytes=mib << 20),
    )


def shape(dims, dtype):
    return jax.ShapeDtypeStruct(dims, dtype)


def chip_shift(x, step, flip=0):
    pairs = []
    for s in range(2 * CHIPS):
        chip, core = s // 2, s % 2
        pairs.append((s, ((chip + step) % CHIPS) * 2 + (core ^ flip)))
    return lax.ppermute(x, "seq", pairs)


def two_way(axes, value, move, count, places, cores=(0, 1)):
    pairs = []
    for index in range(count):
        core = index & 1
        if core in cores:
            pairs.append((index, move(index, places * (1 - 2 * core))))
    return lax.ppermute(value, axes, pairs)


def gather_weight(weight):
    def move(index, step):
        row, place = index // 16, index % 16
        return (row + 4 * step) % 32 * 16 + place

    blocks = []
    for k in range(1, 5):
        cores = (0, 1) if k < 4 else (0,)
        blocks.append(two_way(("rows", "seq"), weight, move, 512, k, cores))
    core = lax.axis_index("seq") & 1
    blocks[3] = jnp.where(core == 0, blocks[3], weight)
    bundle = jnp.concatenate(blocks, axis=0)

    def shift_x(step):
        pairs = [(r, (r & ~3) + ((r + step) & 3)) for r in range(32)]
        return lax.ppermute(bundle, "rows", pairs)

    return [bundle, shift_x(1), shift_x(-1), shift_x(2)]


def body(
    qkv,
    hidden,
    segment_ids,
    key_keep,
    grid_sizes,
    owner_slots,
    out_weight,
    norm_gain,
    norm_bias,
    merge_weight,
):
    del segment_ids
    grid_sizes = jnp.transpose(grid_sizes, (0, 2, 1))
    weight = gather_weight(out_weight)
    packed = call(
        rotary_kernel,
        shape((HEADS, TOK, 256), BF16),
        [SM, VM, VM],
        flops=1 << 22,
        bytes_accessed=1 << 20,
        mib=56,
    )(grid_sizes, key_keep, qkv)
    heads_all = lax.all_to_all(packed, "seq", split_axis=0, concat_axis=0, tiled=True)
    merge_other = chip_shift(merge_weight, 0, 1)
    head_out = call(
        attention_kernel,
        shape((CHIPS, 2, HD // 2, 128), BF16),
        [SM, VM],
        flops=1 << 29,
        bytes_accessed=1 << 20,
    )(grid_sizes, heads_all.reshape(SEQ, 256))
    groups = [[2 * c + p for c in range(CHIPS)] for p in range(2)]
    attended = lax.all_to_all(
        head_out,
        "seq",
        split_axis=0,
        concat_axis=0,
        axis_index_groups=groups,
        tiled=True,
    )
    mixed = call(
        mix_kernel,
        shape((128, D), F32),
        [VM] * 6,
        flops=1 << 28,
        bytes_accessed=3 << 20,
    )(attended, hidden, *weight)
    recv = chip_shift(mixed, 0, 1)
    normed, first, second = call(
        norm_kernel,
        (shape((1, TOK, D), BF16), shape((TOK, D), BF16), shape((TOK, D), BF16)),
        [VM] * 4,
        scratch=[pltpu.VMEM((128, D), BF16)],
        flops=1 << 22,
        bytes_accessed=1 << 20,
    )(mixed, recv, norm_gain, norm_bias)

    def move(index, step):
        return (index + 2 * step) % 16

    def send(value, places):
        return two_way("seq", value, move, 16, places)

    first1, second1 = send(first, 1), send(second, 1)
    first2, second2 = send(first, 2), send(second, 2)
    first3, second3 = send(first1, 2), send(second1, 2)
    first4 = send(first2, 2)
    chunks = [first, first1, second1, first2, second2, first3, second3, first4]
    stats = call(
        project_kernel,
        shape((16, 128), F32),
        [SM, SM] + [VM] * (2 + CHIPS),
        flops=1 << 29,
        bytes_accessed=7 << 20,
        mib=16,
    )(grid_sizes, owner_slots, merge_weight, merge_other, *chunks)
    stats = lax.all_to_all(stats, "seq", split_axis=0, concat_axis=0, tiled=True)
    norm, peak = call(
        final_kernel, (shape((1, 1), F32), shape((1, 1), F32)), [SM, SM, VM]
    )(grid_sizes, owner_slots, stats)
    return (normed, norm, peak)


def solution(mesh):
    placed = (
        P("rows", "seq", None),
        P("rows", "seq", None),
        P("rows", "seq"),
        P("rows", "seq"),
        P("rows", None, None),
        P("rows", None),
        P("rows", None),
        P(),
        P(),
        P(None, "seq"),
    )

    return jax.shard_map(
        body,
        mesh=mesh,
        in_specs=placed,
        out_specs=(P("rows", "seq", None), P("rows", "seq"), P("rows", "seq")),
        check_vma=False,
    )
```

```python
import jax
import jax.numpy as jnp
import numpy as np
from jax import lax
from jax.experimental import pallas as pl
from jax.experimental.pallas import tpu as pltpu
from jax.sharding import PartitionSpec as P


D = 1280
HEADS = 16
HD = 80
OUT = 4096
IMGS = 4
SEQ = 1024
TOK = 64
CHIPS = 8
MAXIMG = 896
NEG = -1e30


F32 = jnp.float32
BF16 = jnp.bfloat16
VM = pl.BlockSpec(memory_space=pltpu.VMEM)
SM = pl.BlockSpec(memory_space=pltpu.SMEM)


def iota(shape, dim):
    return lax.broadcasted_iota(jnp.int32, shape, dim)


def image_bounds(grid_ref):
    starts, ends, total = [], [], 0
    for j in range(IMGS):
        starts.append(total)
        total = total + grid_ref[0, 0, j] * grid_ref[0, 1, j]
        ends.append(total)
    return starts, ends


def rotary_kernel(grid_ref, keep_ref, qkv_ref, out_ref):
    starts, ends = image_bounds(grid_ref)
    place = lax.axis_index("seq") * TOK + iota((TOK, 256), 0)
    begin = jnp.zeros((TOK, 256), jnp.int32)
    width = jnp.full((TOK, 256), 2, jnp.int32)
    for j in range(IMGS):
        inside = (place >= starts[j]) & (place < ends[j])
        begin = jnp.where(inside, starts[j], begin)
        width = jnp.where(inside, grid_ref[0, 1, j], width)
    valid = place < ends[IMGS - 1]
    offset = place - begin
    square = lax.shift_right_logical(offset, 2)
    corner = offset & 3
    half = lax.shift_right_logical(width, 1)
    line = jnp.floor((square.astype(F32) + 0.5) / half.astype(F32)).astype(jnp.int32)
    row = 2 * line + lax.shift_right_logical(corner, 1)
    col = 2 * (square - line * half) + (corner & 1)
    row = jnp.where(valid, row, 0).astype(F32)
    col = jnp.where(valid, col, 0).astype(F32)
    lane = iota((TOK, 256), 1) & 127
    rotated = lane < HD
    pair = lane
    for _ in range(5):
        pair = jnp.where(pair >= 20, pair - 20, pair)
    rate = jnp.exp(pair.astype(F32) * (-np.log(10000.0) / 20))
    angle = jnp.where(lane < HD // 2, row, col) * rate
    cosine = jnp.where(rotated, jnp.cos(angle), 1.0)
    low = (lane < 20) | ((lane >= 40) & (lane < 60))
    sine = jnp.sin(angle)
    sine = jnp.where(rotated, jnp.where(low, -sine, sine), 0.0)
    diagonal = iota((TOK, TOK), 0) == iota((TOK, TOK), 1)
    flags = jnp.where(diagonal, keep_ref[...].astype(F32), 0.0)
    tail = jnp.broadcast_to(jnp.sum(flags, axis=1, keepdims=True), (TOK, 16))
    z = lax.shift_right_logical(lax.axis_index("rows"), 2)
    for head in range(HEADS):
        behind = (z - head // 2) & 7
        ahead = (head // 2 - z) & 7
        low_core = (behind >= 1) & (behind <= 4)
        place = jnp.where(low_core, behind - 1, (ahead + 3) & 3) + 4 * (head % 2)
        dest = 2 * place + jnp.where(low_core, 0, 1)
        q = qkv_ref[0, :, head * HD : head * HD + HD].astype(F32)
        k = qkv_ref[0, :, D + head * HD : D + head * HD + HD].astype(F32)
        v = qkv_ref[0, :, 2 * D + head * HD : 2 * D + head * HD + HD].astype(F32)
        full = jnp.concatenate([q, v[:, :48], k, v[:, 48:], tail], axis=1)
        swapped = jnp.where(low, pltpu.roll(full, 256 - 20, 1), pltpu.roll(full, 20, 1))
        out_ref[dest] = (full * cosine + swapped * sine).astype(BF16)


def attention_kernel(grid_ref, x_ref, out_ref):
    starts, ends = image_bounds(grid_ref)
    pick = jnp.where(iota((8, 128), 1) == 112, 1.0, 0.0).astype(BF16)
    keep = lax.dot_general(
        pick, x_ref[:, 128:], (((1,), (1,)), ((), ())), preferred_element_type=F32
    )[0:1]
    key_place = jnp.where(keep > 0.5, iota((1, SEQ), 1), -1)
    query_lane = iota((128, 128), 1) < HD

    def emit(chip, rows):
        flipped = jnp.transpose(rows)
        out_ref[chip, 0] = flipped[80:120].astype(BF16)
        out_ref[chip, 1] = jnp.concatenate(
            [flipped[120:128], flipped[208:240]], axis=0
        ).astype(BF16)

    for chip in range(MAXIMG // 128):
        first = chip * 128
        low = max(0, first - 256)
        high = min(MAXIMG, first + 384)
        query = jnp.where(query_lane, x_ref[first : first + 128, 0:128], 0)
        scores = lax.dot_general(
            query,
            x_ref[low:high, 128:256],
            (((1,), (1,)), ((), ())),
            preferred_element_type=F32,
        ) * HD ** (-0.5)
        place = first + iota((128, 1), 0)
        lo = place
        hi = place
        for j in range(IMGS):
            inside = (place >= starts[j]) & (place < ends[j])
            lo = jnp.where(inside, starts[j], lo)
            hi = jnp.where(inside, ends[j], hi)
        keys = key_place[:, low:high]
        same = (keys >= lo) & (keys < hi)
        own = iota((1, high - low), 1) + low == place
        scores = jnp.where(same | own, scores, NEG)
        top = jnp.max(scores, axis=1, keepdims=True)
        weights = jnp.exp(scores - top)
        total = jnp.sum(weights, axis=1, keepdims=True)
        summed = jnp.dot(
            weights.astype(BF16), x_ref[low:high, :], preferred_element_type=F32
        )
        emit(chip, summed / total)
    emit(CHIPS - 1, x_ref[MAXIMG:SEQ, :].astype(F32))


def mix_kernel(heads_ref, hidden_ref, own_ref, plus_ref, minus_ref, two_ref, out_ref):
    core = lax.axis_index("seq") & 1
    here = lax.axis_index("rows") & 3
    heads = []
    for step in (0, -1, 1, 2):
        x = (here + step) & 3
        upper, half = lax.shift_right_logical(x, 1), x & 1
        heads += [heads_ref[i + 4 * upper, half] for i in range(4)]
    weight = [ref[...] for ref in (own_ref, plus_ref, minus_ref, two_ref)]
    out_ref[...] = lax.dot_general(
        jnp.concatenate(heads, axis=0),
        jnp.concatenate(weight, axis=0),
        (((0,), (0,)), ((), ())),
        preferred_element_type=F32,
    )
    mine = pl.ds(pl.multiple_of(core * TOK, TOK), TOK)
    out_ref[mine, :] = out_ref[mine, :] + hidden_ref[0].astype(F32)


def norm_kernel(
    own_ref, recv_ref, gain_ref, bias_ref, normed_ref, first_ref, second_ref, keep_ref
):
    mixed = own_ref[...] + recv_ref[...]
    centred = mixed - jnp.mean(mixed, axis=1, keepdims=True)
    spread = jnp.mean(centred * centred, axis=1, keepdims=True)
    normed = centred * lax.rsqrt(spread + 1e-05) * gain_ref[...].reshape(1, D)
    normed = (normed + bias_ref[...].reshape(1, D)).astype(BF16)
    keep_ref[...] = normed
    core = lax.axis_index("seq") & 1
    normed_ref[0] = keep_ref[pl.ds(pl.multiple_of(core * TOK, TOK), TOK), :]
    line = iota((128, 128), 0)
    half = (lax.shift_right_logical(line, 6) + core) & 1
    source = TOK * half + 4 * (line & 15) + (lax.shift_right_logical(line, 4) & 3)
    order = jnp.where(iota((128, 128), 1) == source, 1.0, 0.0).astype(BF16)
    chunks = jnp.dot(order, normed, preferred_element_type=F32).astype(BF16)
    first_ref[...] = chunks[:TOK]
    second_ref[...] = chunks[TOK:]


def project_kernel(grid_ref, owner_ref, wa_ref, wb_ref, *refs):
    out_ref = refs[CHIPS]
    halves = []
    for w_ref in (wa_ref, wb_ref):
        part = 0.0
        for corner in range(4):
            rows = jnp.concatenate(
                [b[16 * corner : 16 * corner + 16, :] for b in refs[:CHIPS]], axis=0
            )
            part = part + jnp.dot(
                rows, w_ref[D * corner : D * corner + D, :], preferred_element_type=F32
            )
        halves.append(part)
    done = jnp.concatenate(halves, axis=1)
    squares = jnp.sum(done * done, axis=1, keepdims=True)
    peaks = jnp.max(done, axis=1, keepdims=True)
    _, ends = image_bounds(grid_ref)
    line = iota((128, 128), 0)
    index = lax.axis_index("seq")
    core = index & 1
    chunk = lax.shift_right_logical(line, 4)
    step = lax.shift_right_logical(chunk + 1, 1)
    second = ((chunk & 1) == 0) & (chunk > 0)
    half = jnp.where(second, 1 - core, core)
    step = jnp.where(core == 0, -step, step)
    source = (lax.shift_right_logical(index, 1) + step) & 7
    token = source * 128 + half * TOK + 4 * (line & 15)
    slot = jnp.full((128, 128), -1, jnp.int32)
    for j in reversed(range(IMGS)):
        slot = jnp.where(token < ends[j], owner_ref[0, j], slot)
    hot = slot == iota((128, 128), 1)
    sums = jnp.sum(jnp.where(hot, squares, 0.0), axis=0, keepdims=True)
    tops = jnp.max(jnp.where(hot, peaks, NEG), axis=0, keepdims=True)
    both = jnp.where(line == 0, sums, jnp.where(line == 1, tops, 0.0))
    out_ref[...] = jnp.transpose(both)[:16]


def final_kernel(grid_ref, owner_ref, stats_ref, norm_ref, peak_ref):
    stats = stats_ref[...]
    total = jnp.sum(stats, axis=0, keepdims=True)[:, 0:1]
    top = jnp.max(stats, axis=0, keepdims=True)[:, 1:2]
    me = lax.axis_index("seq")
    count = 0
    for j in range(IMGS):
        size = lax.shift_right_logical(grid_ref[0, 0, j] * grid_ref[0, 1, j], 2)
        count = count + jnp.where(owner_ref[0, j] == me, size, 0)
    counts = jnp.full((1, 1), count, jnp.int32)
    divisor = (jnp.maximum(counts, 1) * OUT).astype(F32)
    norm_ref[...] = jnp.where(counts > 0, jnp.sqrt(total / divisor + 1e-06), 0.0)
    peak_ref[...] = jnp.where(counts > 0, top, 0.0)


def call(kernel, out, specs, scratch=(), flops=0, bytes_accessed=0, mib=8):
    many = isinstance(out, (tuple, list))
    return pl.pallas_call(
        kernel,
        out_shape=out,
        in_specs=specs,
        out_specs=tuple([VM] * len(out)) if many else VM,
        scratch_shapes=scratch,
        cost_estimate=pl.CostEstimate(
            flops=flops, bytes_accessed=bytes_accessed, transcendentals=0
        ),
        compiler_params=pltpu.CompilerParams(vmem_limit_bytes=mib << 20),
    )


def shape(dims, dtype):
    return jax.ShapeDtypeStruct(dims, dtype)


def chip_shift(x, step, flip=0):
    pairs = []
    for s in range(2 * CHIPS):
        chip, core = s // 2, s % 2
        pairs.append((s, ((chip + step) % CHIPS) * 2 + (core ^ flip)))
    return lax.ppermute(x, "seq", pairs)


def two_way(axes, value, move, count, places, cores=(0, 1)):
    pairs = []
    for index in range(count):
        core = index & 1
        if core in cores:
            pairs.append((index, move(index, places * (1 - 2 * core))))
    return lax.ppermute(value, axes, pairs)


def gather_weight(weight):
    def move(index, step):
        row, place = index // 16, index % 16
        return (row + 4 * step) % 32 * 16 + place

    def send(value, places, cores=(0, 1)):
        return two_way(("rows", "seq"), value, move, 512, places, cores)

    one = send(weight, 1)
    four = send(weight, 4, (0,))
    two = send(jnp.concatenate([weight, one], axis=0), 2)
    core = lax.axis_index("seq") & 1
    bundle = jnp.concatenate([one, two, jnp.where(core == 0, four, weight)], axis=0)

    def shift_x(step):
        pairs = [(r, (r & ~3) + ((r + step) & 3)) for r in range(32)]
        return lax.ppermute(bundle, "rows", pairs)

    return [bundle, shift_x(1), shift_x(-1), shift_x(2)]


def body(
    qkv,
    hidden,
    segment_ids,
    key_keep,
    grid_sizes,
    owner_slots,
    out_weight,
    norm_gain,
    norm_bias,
    merge_weight,
):
    del segment_ids
    grid_sizes = jnp.transpose(grid_sizes, (0, 2, 1))
    weight = gather_weight(out_weight)
    packed = call(
        rotary_kernel,
        shape((HEADS, TOK, 256), BF16),
        [SM, VM, VM],
        flops=1 << 22,
        bytes_accessed=1 << 20,
        mib=56,
    )(grid_sizes, key_keep, qkv)
    heads_all = lax.all_to_all(packed, "seq", split_axis=0, concat_axis=0, tiled=True)
    merge_other = chip_shift(merge_weight, 0, 1)
    head_out = call(
        attention_kernel,
        shape((CHIPS, 2, HD // 2, 128), BF16),
        [SM, VM],
        flops=1 << 29,
        bytes_accessed=1 << 20,
    )(grid_sizes, heads_all.reshape(SEQ, 256))
    groups = [[2 * c + p for c in range(CHIPS)] for p in range(2)]
    attended = lax.all_to_all(
        head_out,
        "seq",
        split_axis=0,
        concat_axis=0,
        axis_index_groups=groups,
        tiled=True,
    )
    mixed = call(
        mix_kernel,
        shape((128, D), F32),
        [VM] * 6,
        flops=1 << 28,
        bytes_accessed=3 << 20,
    )(attended, hidden, *weight)
    recv = chip_shift(mixed, 0, 1)
    normed, first, second = call(
        norm_kernel,
        (shape((1, TOK, D), BF16), shape((TOK, D), BF16), shape((TOK, D), BF16)),
        [VM] * 4,
        scratch=[pltpu.VMEM((128, D), BF16)],
        flops=1 << 22,
        bytes_accessed=1 << 20,
    )(mixed, recv, norm_gain, norm_bias)

    def move(index, step):
        return (index + 2 * step) % 16

    def send(value, places):
        return two_way("seq", value, move, 16, places)

    first1, second1 = send(first, 1), send(second, 1)
    first2, second2 = send(first, 2), send(second, 2)
    first3, second3 = send(first1, 2), send(second1, 2)
    first4 = send(first2, 2)
    chunks = [first, first1, second1, first2, second2, first3, second3, first4]
    stats = call(
        project_kernel,
        shape((16, 128), F32),
        [SM, SM] + [VM] * (2 + CHIPS),
        flops=1 << 29,
        bytes_accessed=7 << 20,
        mib=16,
    )(grid_sizes, owner_slots, merge_weight, merge_other, *chunks)
    stats = lax.all_to_all(stats, "seq", split_axis=0, concat_axis=0, tiled=True)
    norm, peak = call(
        final_kernel, (shape((1, 1), F32), shape((1, 1), F32)), [SM, SM, VM]
    )(grid_sizes, owner_slots, stats)
    return (normed, norm, peak)


def solution(mesh):
    placed = (
        P("rows", "seq", None),
        P("rows", "seq", None),
        P("rows", "seq"),
        P("rows", "seq"),
        P("rows", None, None),
        P("rows", None),
        P("rows", None),
        P(),
        P(),
        P(None, "seq"),
    )

    return jax.shard_map(
        body,
        mesh=mesh,
        in_specs=placed,
        out_specs=(P("rows", "seq", None), P("rows", "seq"), P("rows", "seq")),
        check_vma=False,
    )
```

```python
import jax
import jax.numpy as jnp
import numpy as np
from jax import lax
from jax.experimental import pallas as pl
from jax.experimental.pallas import tpu as pltpu
from jax.sharding import PartitionSpec as P


D = 1280
HEADS = 16
HD = 80
OUT = 4096
IMGS = 4
SEQ = 1024
TOK = 64
CHIPS = 8
MAXIMG = 896
NEG = -1e30


F32 = jnp.float32
BF16 = jnp.bfloat16
VM = pl.BlockSpec(memory_space=pltpu.VMEM)
SM = pl.BlockSpec(memory_space=pltpu.SMEM)


def iota(shape, dim):
    return lax.broadcasted_iota(jnp.int32, shape, dim)


def image_bounds(grid_ref):
    starts, ends, total = [], [], 0
    for j in range(IMGS):
        starts.append(total)
        total = total + grid_ref[0, 0, j] * grid_ref[0, 1, j]
        ends.append(total)
    return starts, ends


def rotary_kernel(grid_ref, keep_ref, qkv_ref, out_ref):
    starts, ends = image_bounds(grid_ref)
    place = lax.axis_index("seq") * TOK + iota((TOK, 256), 0)
    begin = jnp.zeros((TOK, 256), jnp.int32)
    width = jnp.full((TOK, 256), 2, jnp.int32)
    end = jnp.zeros((TOK, 256), jnp.int32)
    for j in range(IMGS):
        inside = (place >= starts[j]) & (place < ends[j])
        begin = jnp.where(inside, starts[j], begin)
        width = jnp.where(inside, grid_ref[0, 1, j], width)
        end = jnp.where(inside, ends[j], end)
    valid = place < ends[IMGS - 1]
    offset = place - begin
    square = lax.shift_right_logical(offset, 2)
    corner = offset & 3
    half = lax.shift_right_logical(width, 1)
    line = jnp.floor((square.astype(F32) + 0.5) / half.astype(F32)).astype(jnp.int32)
    row = 2 * line + lax.shift_right_logical(corner, 1)
    col = 2 * (square - line * half) + (corner & 1)
    row = jnp.where(valid, row, 0).astype(F32)
    col = jnp.where(valid, col, 0).astype(F32)
    lane = iota((TOK, 256), 1) & 127
    rotated = lane < HD
    pair = lane
    for _ in range(5):
        pair = jnp.where(pair >= 20, pair - 20, pair)
    rate = jnp.exp(pair.astype(F32) * (-np.log(10000.0) / 20))
    angle = jnp.where(lane < HD // 2, row, col) * rate
    cosine = jnp.where(rotated, jnp.cos(angle), 1.0)
    low = (lane < 20) | ((lane >= 40) & (lane < 60))
    sine = jnp.sin(angle)
    sine = jnp.where(rotated, jnp.where(low, -sine, sine), 0.0)
    diagonal = iota((TOK, TOK), 0) == iota((TOK, TOK), 1)
    flags = jnp.where(diagonal, keep_ref[...].astype(F32), 0.0)
    spare = iota((TOK, 16), 1)
    tail = jnp.where(spare == 0, jnp.sum(flags, axis=1, keepdims=True), 0.0)
    tail = jnp.where(spare == 1, 0.25 * begin[:, :16].astype(F32), tail)
    tail = jnp.where(spare == 2, 0.25 * end[:, :16].astype(F32), tail)
    z = lax.shift_right_logical(lax.axis_index("rows"), 2)
    for head in range(HEADS):
        behind = (z - head // 2) & 7
        ahead = (head // 2 - z) & 7
        low_core = (behind >= 1) & (behind <= 4)
        place = jnp.where(low_core, behind - 1, (ahead + 3) & 3) + 4 * (head % 2)
        dest = 2 * place + jnp.where(low_core, 0, 1)
        q = qkv_ref[0, :, head * HD : head * HD + HD].astype(F32)
        k = qkv_ref[0, :, D + head * HD : D + head * HD + HD].astype(F32)
        v = qkv_ref[0, :, 2 * D + head * HD : 2 * D + head * HD + HD].astype(F32)
        full = jnp.concatenate([q, v[:, :48], k, v[:, 48:], tail], axis=1)
        swapped = jnp.where(low, pltpu.roll(full, 256 - 20, 1), pltpu.roll(full, 20, 1))
        out_ref[dest] = (full * cosine + swapped * sine).astype(BF16)


def attention_kernel(x_ref, out_ref):
    pick = jnp.where(iota((8, 128), 1) == 112, 1.0, 0.0).astype(BF16)
    keep = lax.dot_general(
        pick, x_ref[:, 128:], (((1,), (1,)), ((), ())), preferred_element_type=F32
    )[0:1]
    key_place = jnp.where(keep > 0.5, iota((1, SEQ), 1).astype(F32), -1.0)
    query_lane = iota((128, 128), 1) < HD

    def emit(chip, rows):
        flipped = jnp.transpose(rows)
        out_ref[chip, 0] = flipped[80:120].astype(BF16)
        out_ref[chip, 1] = jnp.concatenate(
            [flipped[120:128], flipped[208:240]], axis=0
        ).astype(BF16)

    for chip in range(MAXIMG // 128):
        first = chip * 128
        low = max(0, first - 256)
        high = min(MAXIMG, first + 384)
        query = jnp.where(query_lane, x_ref[first : first + 128, 0:128], 0)
        scores = lax.dot_general(
            query,
            x_ref[low:high, 128:256],
            (((1,), (1,)), ((), ())),
            preferred_element_type=F32,
        ) * HD ** (-0.5)
        place = first + iota((128, 1), 0)
        bounds = 4.0 * x_ref[first : first + 128, 128:256].astype(F32)
        lo, hi = bounds[:, 113:114], bounds[:, 114:115]
        keys = key_place[:, low:high]
        same = (keys >= lo) & (keys < hi)
        own = iota((1, high - low), 1) + low == place
        scores = jnp.where(same | own, scores, NEG)
        top = jnp.max(scores, axis=1, keepdims=True)
        weights = jnp.exp(scores - top)
        total = jnp.sum(weights, axis=1, keepdims=True)
        summed = jnp.dot(
            weights.astype(BF16), x_ref[low:high, :], preferred_element_type=F32
        )
        emit(chip, summed / total)
    emit(CHIPS - 1, x_ref[MAXIMG:SEQ, :].astype(F32))


def mix_kernel(heads_ref, hidden_ref, own_ref, plus_ref, minus_ref, two_ref, out_ref):
    core = lax.axis_index("seq") & 1
    here = lax.axis_index("rows") & 3
    heads = []
    for step in (0, -1, 1, 2):
        x = (here + step) & 3
        upper, half = lax.shift_right_logical(x, 1), x & 1
        heads += [heads_ref[i + 4 * upper, half] for i in range(4)]
    weight = [ref[...] for ref in (own_ref, plus_ref, minus_ref, two_ref)]
    out_ref[...] = lax.dot_general(
        jnp.concatenate(heads, axis=0),
        jnp.concatenate(weight, axis=0),
        (((0,), (0,)), ((), ())),
        preferred_element_type=F32,
    )
    mine = pl.ds(pl.multiple_of(core * TOK, TOK), TOK)
    out_ref[mine, :] = out_ref[mine, :] + hidden_ref[0].astype(F32)


def norm_kernel(
    own_ref, recv_ref, gain_ref, bias_ref, normed_ref, block_ref, keep_ref
):
    mixed = own_ref[...] + recv_ref[...]
    centred = mixed - jnp.mean(mixed, axis=1, keepdims=True)
    spread = jnp.mean(centred * centred, axis=1, keepdims=True)
    normed = centred * lax.rsqrt(spread + 1e-05) * gain_ref[...].reshape(1, D)
    normed = (normed + bias_ref[...].reshape(1, D)).astype(BF16)
    keep_ref[...] = normed
    core = lax.axis_index("seq") & 1
    normed_ref[0] = keep_ref[pl.ds(pl.multiple_of(core * TOK, TOK), TOK), :]
    line = iota((128, 128), 0)
    half = (lax.shift_right_logical(line, 6) + core) & 1
    source = TOK * half + 4 * (line & 15) + (lax.shift_right_logical(line, 4) & 3)
    order = jnp.where(iota((128, 128), 1) == source, 1.0, 0.0).astype(BF16)
    block_ref[...] = jnp.dot(order, normed, preferred_element_type=F32).astype(BF16)


def project_kernel(grid_ref, owner_ref, wa_ref, wb_ref, *refs):
    own_ref, one_ref, two_ref, three_ref, four_ref, out_ref = refs
    chunks = [(own_ref, 0), (one_ref, 0), (one_ref, TOK), (two_ref, 0), (two_ref, TOK)]
    chunks += [(three_ref, 0), (three_ref, TOK), (four_ref, 0)]
    halves = []
    for w_ref in (wa_ref, wb_ref):
        part = 0.0
        for corner in range(4):
            rows = jnp.concatenate(
                [ref[pl.ds(at + 16 * corner, 16), :] for ref, at in chunks], axis=0
            )
            part = part + jnp.dot(
                rows, w_ref[D * corner : D * corner + D, :], preferred_element_type=F32
            )
        halves.append(part)
    done = jnp.concatenate(halves, axis=1)
    squares = jnp.sum(done * done, axis=1, keepdims=True)
    peaks = jnp.max(done, axis=1, keepdims=True)
    _, ends = image_bounds(grid_ref)
    line = iota((128, 128), 0)
    index = lax.axis_index("seq")
    core = index & 1
    chunk = lax.shift_right_logical(line, 4)
    step = lax.shift_right_logical(chunk + 1, 1)
    second = ((chunk & 1) == 0) & (chunk > 0)
    half = jnp.where(second, 1 - core, core)
    step = jnp.where(core == 0, -step, step)
    source = (lax.shift_right_logical(index, 1) + step) & 7
    token = source * 128 + half * TOK + 4 * (line & 15)
    slot = jnp.full((128, 128), -1, jnp.int32)
    for j in reversed(range(IMGS)):
        slot = jnp.where(token < ends[j], owner_ref[0, j], slot)
    hot = slot == iota((128, 128), 1)
    sums = jnp.sum(jnp.where(hot, squares, 0.0), axis=0, keepdims=True)
    tops = jnp.max(jnp.where(hot, peaks, NEG), axis=0, keepdims=True)
    both = jnp.where(line == 0, sums, jnp.where(line == 1, tops, 0.0))
    out_ref[...] = jnp.transpose(both)[:16]


def final_kernel(grid_ref, owner_ref, stats_ref, norm_ref, peak_ref):
    stats = stats_ref[...]
    total = jnp.sum(stats, axis=0, keepdims=True)[:, 0:1]
    top = jnp.max(stats, axis=0, keepdims=True)[:, 1:2]
    me = lax.axis_index("seq")
    count = 0
    for j in range(IMGS):
        size = lax.shift_right_logical(grid_ref[0, 0, j] * grid_ref[0, 1, j], 2)
        count = count + jnp.where(owner_ref[0, j] == me, size, 0)
    counts = jnp.full((1, 1), count, jnp.int32)
    divisor = (jnp.maximum(counts, 1) * OUT).astype(F32)
    norm_ref[...] = jnp.where(counts > 0, jnp.sqrt(total / divisor + 1e-06), 0.0)
    peak_ref[...] = jnp.where(counts > 0, top, 0.0)


def call(kernel, out, specs, scratch=(), flops=0, bytes_accessed=0, mib=8):
    many = isinstance(out, (tuple, list))
    return pl.pallas_call(
        kernel,
        out_shape=out,
        in_specs=specs,
        out_specs=tuple([VM] * len(out)) if many else VM,
        scratch_shapes=scratch,
        cost_estimate=pl.CostEstimate(
            flops=flops, bytes_accessed=bytes_accessed, transcendentals=0
        ),
        compiler_params=pltpu.CompilerParams(vmem_limit_bytes=mib << 20),
    )


def shape(dims, dtype):
    return jax.ShapeDtypeStruct(dims, dtype)


def chip_shift(x, step, flip=0):
    pairs = []
    for s in range(2 * CHIPS):
        chip, core = s // 2, s % 2
        pairs.append((s, ((chip + step) % CHIPS) * 2 + (core ^ flip)))
    return lax.ppermute(x, "seq", pairs)


def two_way(axes, value, move, count, places, cores=(0, 1)):
    pairs = []
    for index in range(count):
        core = index & 1
        if core in cores:
            pairs.append((index, move(index, places * (1 - 2 * core))))
    return lax.ppermute(value, axes, pairs)


def gather_weight(weight):
    def move(index, step):
        row, place = index // 16, index % 16
        return (row + 4 * step) % 32 * 16 + place

    def send(value, places, cores=(0, 1)):
        return two_way(("rows", "seq"), value, move, 512, places, cores)

    one = send(weight, 1)
    four = send(weight, 4, (0,))
    two = send(jnp.concatenate([weight, one], axis=0), 2)
    core = lax.axis_index("seq") & 1
    bundle = jnp.concatenate([one, two, jnp.where(core == 0, four, weight)], axis=0)

    def shift_x(step):
        pairs = [(r, (r & ~3) + ((r + step) & 3)) for r in range(32)]
        return lax.ppermute(bundle, "rows", pairs)

    return [bundle, shift_x(1), shift_x(-1), shift_x(2)]


def body(
    qkv,
    hidden,
    segment_ids,
    key_keep,
    grid_sizes,
    owner_slots,
    out_weight,
    norm_gain,
    norm_bias,
    merge_weight,
):
    del segment_ids
    grid_sizes = jnp.transpose(grid_sizes, (0, 2, 1))
    weight = gather_weight(out_weight)
    packed = call(
        rotary_kernel,
        shape((HEADS, TOK, 256), BF16),
        [SM, VM, VM],
        flops=1 << 22,
        bytes_accessed=1 << 20,
        mib=56,
    )(grid_sizes, key_keep, qkv)
    heads_all = lax.all_to_all(packed, "seq", split_axis=0, concat_axis=0, tiled=True)
    merge_other = chip_shift(merge_weight, 0, 1)
    head_out = call(
        attention_kernel,
        shape((CHIPS, 2, HD // 2, 128), BF16),
        [VM],
        flops=1 << 29,
        bytes_accessed=1 << 20,
    )(heads_all.reshape(SEQ, 256))
    groups = [[2 * c + p for c in range(CHIPS)] for p in range(2)]
    attended = lax.all_to_all(
        head_out,
        "seq",
        split_axis=0,
        concat_axis=0,
        axis_index_groups=groups,
        tiled=True,
    )
    mixed = call(
        mix_kernel,
        shape((128, D), F32),
        [VM] * 6,
        flops=1 << 28,
        bytes_accessed=3 << 20,
    )(attended, hidden, *weight)
    recv = chip_shift(mixed, 0, 1)
    normed, block = call(
        norm_kernel,
        (shape((1, TOK, D), BF16), shape((128, D), BF16)),
        [VM] * 4,
        scratch=[pltpu.VMEM((128, D), BF16)],
        flops=1 << 22,
        bytes_accessed=1 << 20,
    )(mixed, recv, norm_gain, norm_bias)

    def move(index, step):
        return (index + 2 * step) % 16

    def send(value, places):
        return two_way("seq", value, move, 16, places)

    one, two = send(block, 1), send(block, 2)
    three, four = send(one, 2), send(one[:TOK], 3)
    chunks = [block, one, two, three, four]
    stats = call(
        project_kernel,
        shape((16, 128), F32),
        [SM, SM] + [VM] * 7,
        flops=1 << 29,
        bytes_accessed=7 << 20,
        mib=16,
    )(grid_sizes, owner_slots, merge_weight, merge_other, *chunks)
    stats = lax.all_to_all(stats, "seq", split_axis=0, concat_axis=0, tiled=True)
    norm, peak = call(
        final_kernel, (shape((1, 1), F32), shape((1, 1), F32)), [SM, SM, VM]
    )(grid_sizes, owner_slots, stats)
    return (normed, norm, peak)


def solution(mesh):
    placed = (
        P("rows", "seq", None),
        P("rows", "seq", None),
        P("rows", "seq"),
        P("rows", "seq"),
        P("rows", None, None),
        P("rows", None),
        P("rows", None),
        P(),
        P(),
        P(None, "seq"),
    )

    return jax.shard_map(
        body,
        mesh=mesh,
        in_specs=placed,
        out_specs=(P("rows", "seq", None), P("rows", "seq"), P("rows", "seq")),
        check_vma=False,
    )
```
